512 devices in a mesh: rows: 64 (over y, z), cols: 8 (over x, core).
Axes of the slice: x: 4, y: 8, z: 8, core: 2. Of those that a mesh axis runs over, the one named last changes fastest.
Arguments:
- patches: bfloat16 [512, 512, 512], P('rows', 'cols'), may hold values from -6 to 6
- tissue: int32 [512, 512], P('rows', 'cols'), may hold values 0 or 1
- w_value: bfloat16 [512, 512], replicated, may hold values from -0.25 to 0.25
- w_across: bfloat16 [512, 40], replicated, may hold values from -0.25 to 0.25
- w_down: bfloat16 [512, 40], replicated, may hold values from -0.25 to 0.25
- w_gate: bfloat16 [512, 512], replicated, may hold values from -0.25 to 0.25
- w_out: bfloat16 [512, 512], replicated, may hold values from -0.25 to 0.25
- step_bias_across: float32 [8], replicated, may hold values from -4.5 to -2.5
- step_bias_down: float32 [8], replicated, may hold values from -4.5 to -2.5
- rates_across: float32 [8], replicated, may hold values from 0.00390625 to 1
- rates_down: float32 [8], replicated, may hold values from 0.00390625 to 1
- skip_across: float32 [8], replicated, may hold values from 0.5 to 1.5
- skip_down: float32 [8], replicated, may hold values from 0.5 to 1.5
- gain_across: float32 [512], replicated, may hold values from 0.5 to 1.5
- gain_final: float32 [512], replicated, may hold values from 0.5 to 1.5
Outputs:
- mixed: bfloat16 [512, 512, 512], P('rows', 'cols')
The draws below stay inside these ranges and needn't reach their ends.
Inputs may be any that keep to these rules, and one draw needn't show every extreme that they name: 1 marks a tissue patch, 0 background.
All inputs are finite; a program needn't handle non-finite values. No bound on the sum of `tissue` on one device may be relied on, other than what follows from the above.
Results may differ from the reference program's by a relative error of at most 0.015.
Values may be sent and summed in bfloat16 or wider, within the bound.
No kernel may reach another device: no remote copies, remote signals or barrier semaphores. Data moves between devices by JAX's collectives and lax.ppermute only.
A program may use at most 64 MiB of HBM per device.

```python
import math
import jax
import jax.numpy as jnp
from jax import lax

HEADS = 8
D = 512
PROJ = 40
H = 512
W = 512


def set_ends(result, rng, low, high):
    longest = result.shape.index(max(result.shape))
    spots = []
    for shift in (0, 1):
        where = [jax.random.randint(jax.random.fold_in(rng, axis), (), 0, length) for axis, length in enumerate(result.shape)]
        where[longest] = (where[longest] + shift) % result.shape[longest]
        spots.append(tuple(where))
    return result.at[spots[0]].set(low).at[spots[1]].set(high)


def level_of(key, extent, shards, smallest, high):
    def one(dim, shards_of):
        draws = jax.random.uniform(jax.random.fold_in(jax.random.fold_in(key, 6), dim), (shards_of,), jnp.float32, smallest / len(shards), high / len(shards))
        return jnp.repeat(jnp.exp(draws), extent[dim] // shards_of).reshape((-1,) + (1,) * (len(extent) - dim - 1))

    factor_of = one(*shards[0])
    for cut in shards[1:]:
        factor_of = factor_of * one(*cut)
    return factor_of


def scatter_about(stream_key, dims, width, bound, split=(), dtype=jnp.bfloat16):
    entries = width * jax.random.normal(stream_key, dims, jnp.float32)
    if split:
        entries = entries * level_of(stream_key, dims, split, -0.22, 0.18)
    return jnp.clip(entries, -bound, bound).astype(dtype)


def setup_inputs(seed: int = 0) -> dict:
    streams_of = jax.random.split(jax.random.key(seed), 16)
    return {
        "patches": scatter_about(streams_of[0], (H, W, D), 1.0, 6.0, ((0, 64), (1, 8))),
        "tissue": set_ends((jax.random.randint(streams_of[1], (H, W), 0, 4) < 3).astype(jnp.int32), jax.random.fold_in(streams_of[1], 1), 0, 1),
        "w_value": scatter_about(streams_of[2], (D, D), D ** -0.5, 0.25),
        "w_across": scatter_about(streams_of[3], (D, PROJ), D ** -0.5, 0.25),
        "w_down": scatter_about(streams_of[4], (D, PROJ), D ** -0.5, 0.25),
        "w_gate": scatter_about(streams_of[5], (D, D), D ** -0.5, 0.25),
        "w_out": scatter_about(streams_of[6], (D, D), D ** -0.5, 0.25),
        "step_bias_across": jnp.clip(jax.random.uniform(streams_of[7], (HEADS,), jnp.float32, -4.5, -2.5), -4.5, -2.5),
        "step_bias_down": jnp.clip(jax.random.uniform(streams_of[8], (HEADS,), jnp.float32, -4.5, -2.5), -4.5, -2.5),
        "rates_across": jnp.clip(jnp.exp(jax.random.uniform(streams_of[9], (HEADS,), jnp.float32, math.log(0.00390625), math.log(1.0))), 0.00390625, 1.0),
        "rates_down": jnp.clip(jnp.exp(jax.random.uniform(streams_of[10], (HEADS,), jnp.float32, math.log(0.00390625), math.log(1.0))), 0.00390625, 1.0),
        "skip_across": jnp.clip(jax.random.uniform(streams_of[11], (HEADS,), jnp.float32, 0.5, 1.5), 0.5, 1.5),
        "skip_down": jnp.clip(jax.random.uniform(streams_of[12], (HEADS,), jnp.float32, 0.5, 1.5), 0.5, 1.5),
        "gain_across": jnp.clip(1.0 + 0.1 * jax.random.normal(streams_of[13], (D,), jnp.float32), 0.5, 1.5),
        "gain_final": jnp.clip(1.0 + 0.1 * jax.random.normal(streams_of[14], (D,), jnp.float32), 0.5, 1.5),
    }


highest = lax.Precision.HIGHEST

def rounded(values):
    return lax.optimization_barrier(values.astype(jnp.bfloat16)).astype(jnp.float32)

def scan_parts(values, b_rows, c_rows, step_sizes, rates, skips):
    line_count, length, head_count, head_width = values.shape
    state_count = b_rows.shape[-1]
    block_len = math.gcd(length, 128)
    block_count = length // block_len
    inputs = values.astype(jnp.float32).reshape(line_count, block_count, block_len, head_count, head_width)
    b_blocks = b_rows.reshape(line_count, block_count, block_len, state_count)
    c_blocks = c_rows.reshape(line_count, block_count, block_len, state_count)
    step_blocks = step_sizes.reshape(line_count, block_count, block_len, head_count)
    running = jnp.cumsum(-step_blocks * rates, axis=2)
    causal = (jnp.arange(block_len)[:, None] >= jnp.arange(block_len)[None, :])[None, None, :, :, None]
    spans = jnp.where(causal, running[:, :, :, None, :] - running[:, :, None, :, :], 0.0)
    decays = jnp.where(causal, jnp.exp(spans), 0.0)
    intersections = jnp.einsum('lctn,lcsn->lcts', c_blocks, b_blocks, precision=highest)
    weights = rounded(decays * intersections[..., None] * step_blocks[:, :, None, :, :])
    within = jnp.einsum('lctsh,lcshp->lcthp', weights, inputs, precision=highest)
    to_end = jnp.exp(running[:, :, -1:, :] - running) * step_blocks
    push_coef = rounded(b_blocks[..., :, None] * to_end[..., None, :])
    pushed = jnp.einsum('lcsnh,lcshp->lchnp', push_coef, inputs, precision=highest)
    totals = running[:, :, -1, :]

    def advance(entered, item):
        pushed_one, total_one = item
        return (jnp.exp(total_one)[..., None, None] * entered + pushed_one, entered)
    final, entering = lax.scan(advance, jnp.zeros_like(pushed[:, 0]), (jnp.moveaxis(pushed, 1, 0), jnp.moveaxis(totals, 1, 0)))
    entering = jnp.moveaxis(entering, 0, 1)
    carried = jnp.einsum('lctn,lchnp->lcthp', c_blocks, entering, precision=highest) * jnp.exp(running)[..., None]
    outputs = within + carried + skips[:, None] * inputs
    return outputs.reshape(line_count, length, head_count * head_width)

def line_scan(values, projected, step_bias, rates, skips):
    head_count = rates.shape[0]
    state_count = (projected.shape[-1] - head_count) // 2
    line_count, length, width_all = values.shape
    b_rows = projected[..., :state_count]
    c_rows = projected[..., state_count:2 * state_count]
    step_sizes = jax.nn.softplus(projected[..., 2 * state_count:] + step_bias)
    return scan_parts(values.reshape(line_count, length, head_count, width_all // head_count), b_rows, c_rows, step_sizes, rates, skips)

def rms_norm(values, gain):
    return values * lax.rsqrt(lax.optimization_barrier(jnp.mean(values * values, axis=-1, keepdims=True)) + 1e-05) * gain

def reference(patches, tissue, w_value, w_across, w_down, w_gate, w_out, step_bias_across, step_bias_down, rates_across, rates_down, skip_across, skip_down, gain_across, gain_final):
    masked = patches * tissue.astype(jnp.bfloat16)[..., None]
    row_total, col_total, feature_count = masked.shape
    row_group = math.gcd(row_total, 16)

    def across(row_block):
        values_across = jnp.dot(row_block, w_value, preferred_element_type=jnp.float32).astype(jnp.bfloat16)
        proj_across = jnp.dot(row_block, w_across, preferred_element_type=jnp.float32)
        y_across = line_scan(values_across, proj_across, step_bias_across, rates_across, skip_across)
        return rms_norm(y_across, gain_across).astype(jnp.bfloat16)
    line_out = lax.map(across, masked.reshape(row_total // row_group, row_group, col_total, feature_count)).reshape(masked.shape)
    columns = jnp.swapaxes(line_out, 0, 1)
    col_group = math.gcd(col_total, 8)

    def downward(col_block):
        proj_down = jnp.dot(col_block, w_down, preferred_element_type=jnp.float32)
        y_down = line_scan(col_block, proj_down, step_bias_down, rates_down, skip_down)
        return y_down.astype(jnp.bfloat16)
    column_out = lax.map(downward, columns.reshape(col_total // col_group, col_group, row_total, feature_count))
    column_out = jnp.swapaxes(column_out.reshape(col_total, row_total, feature_count), 0, 1)
    gate = jnp.dot(masked, w_gate, preferred_element_type=jnp.float32)
    act = (rms_norm(column_out.astype(jnp.float32), gain_final) * jax.nn.silu(gate)).astype(jnp.bfloat16)
    return (masked.astype(jnp.float32) + jnp.dot(act, w_out, preferred_element_type=jnp.float32)).astype(jnp.bfloat16)
```

```python
import jax
import jax.numpy as jnp
from jax import lax
from jax.experimental import pallas as pl
from jax.experimental.pallas import tpu as pltpu
from jax.sharding import PartitionSpec as P

highest = lax.Precision.HIGHEST
bf16, f32 = jnp.bfloat16, jnp.float32
LANES = 128
CAP = 80.0


def iota(shape, dim):
    return lax.broadcasted_iota(jnp.int32, shape, dim)


def dot(a, b, precision=None):
    return jnp.dot(a, b, preferred_element_type=f32, precision=precision)


def halves(x):
    high = x.astype(bf16)
    return high, (x - high.astype(f32)).astype(bf16)


def softplus(v):
    return jnp.maximum(v, 0.0) + jnp.log1p(jnp.exp(-jnp.abs(v)))


def as_column(row):
    n = row.shape[-1]
    square = jnp.broadcast_to(row, (n, n))
    return jnp.sum(jnp.where(iota((n, n), 0) == iota((n, n), 1), square, 0.0), axis=1, keepdims=True)


def head_lanes(head_count, width):
    shape = (head_count, head_count * width)
    return jnp.where(iota(shape, 1) // width == iota(shape, 0), 1.0, 0.0)


def step_terms(proj_rows, bias, rates, group):
    head_count = bias.shape[-1]
    steps = softplus(proj_rows[-head_count:] + as_column(bias))
    falls = -steps * as_column(rates)
    logs = jnp.log(steps)
    blocks = proj_rows.shape[1] // LANES
    stack = lambda x: jnp.concatenate([x[:, k * LANES : (k + 1) * LANES] for k in range(blocks)], axis=0)
    falls, logs = stack(falls), stack(logs)
    source, target = iota((LANES, LANES), 0), iota((LANES, LANES), 1)
    same = source // group == target // group
    running = dot(falls, jnp.where(same & (source <= target), 1.0, 0.0), highest)
    totals = dot(falls, jnp.where(same, 1.0, 0.0), highest)
    return running, running - logs, totals


def products(proj_block, b_block):
    state_count = b_block.shape[0]
    rest = proj_block.shape[1] - 2 * state_count
    padded = jnp.concatenate(
        [jnp.zeros_like(b_block), b_block, jnp.zeros((rest, b_block.shape[1]), f32)], axis=0
    )
    return dot(proj_block, padded, highest)


def within(proj_block, b_block, group, run_col, less_row, values, block, head_count):
    source, target = iota((LANES, LANES), 1), iota((LANES, LANES), 0)
    keep = (source // group == target // group) & (source <= target)
    inter = jnp.where(keep, products(proj_block, b_block), 0.0)
    low_lanes = iota((LANES, LANES), 1) < LANES // 2
    tiles = []
    for pair in range(head_count // 2):
        weights = []
        for head in (2 * pair, 2 * pair + 1):
            at = block * head_count + head
            spans = run_col[:, at : at + 1] - less_row[at : at + 1, :]
            weights.append((jnp.exp(jnp.minimum(spans, CAP)) * inter).astype(bf16))
        both = dot(jnp.concatenate(weights, axis=0), values[:, pair * LANES : (pair + 1) * LANES])
        tiles.append(jnp.where(low_lanes, both[:LANES], both[LANES:]))
    return jnp.concatenate(tiles, axis=1)


def pushes(b_block, to_end, group, values, block, head_count):
    state_count = b_block.shape[0]
    groups = LANES // group
    lane = iota((state_count, LANES), 1)
    tiles = [[] for _ in range(groups)]
    for pair in range(head_count // 2):
        rows = []
        for g in range(groups):
            for head in (2 * pair, 2 * pair + 1):
                at = block * head_count + head
                coef = b_block * to_end[at : at + 1, :]
                rows.append(jnp.where(lane // group == g, coef, 0.0).astype(bf16))
        left = dot(jnp.concatenate(rows, axis=0), values[:, pair * LANES : (pair + 1) * LANES])
        for g in range(groups):
            top = left[2 * g * state_count : (2 * g + 1) * state_count]
            bottom = left[(2 * g + 1) * state_count : (2 * g + 2) * state_count]
            tiles[g].append(jnp.where(lane < LANES // 2, top, bottom))
    return [jnp.concatenate(t, axis=1) for t in tiles]


def prepare(patches, tissue, w_value, w_proj, bias, rates, masked, values, proj, b_rows, run_col, less_row, payload):
    line_count, width = tissue.shape
    head_count = bias.shape[-1]
    flags = jnp.transpose(tissue[...].astype(f32))
    for r in range(line_count):
        keep = jnp.broadcast_to(flags[:, r : r + 1], (width, patches.shape[1])).astype(bf16)
        rows = slice(r * width, (r + 1) * width)
        masked[rows, :] = patches[rows, :] * keep
    inputs = masked[...]
    narrow = dot(inputs, w_value[...]).astype(bf16)
    values[...] = narrow
    proj[...] = dot(inputs, w_proj[...])
    proj_rows = lax.dot_general(
        w_proj[...], inputs, (((0,), (1,)), ((), ())), preferred_element_type=f32
    )
    state_count = (proj.shape[1] - head_count) // 2
    b_rows[...] = proj_rows[:state_count]
    running, less, totals = step_terms(proj_rows, bias[...], rates[...], width)
    less_row[...] = less
    run_col[...] = jnp.transpose(running)
    to_end = jnp.exp(totals - less)
    total_cols = jnp.transpose(totals)
    blocks = inputs.shape[0] // LANES
    groups = LANES // width
    shape = (line_count, blocks * head_count)
    line, column = iota(shape, 0), iota(shape, 1)
    picked = jnp.zeros(shape, f32)
    for g in range(groups):
        here = (line % groups == g) & (column // head_count == line // groups)
        picked = jnp.where(here, total_cols[g * width : g * width + 1, :], picked)
    lanes = jnp.concatenate([head_lanes(head_count, inputs.shape[1] // head_count)] * blocks, axis=0)
    decays = jnp.exp(dot(picked, lanes, highest))
    high, low = halves(decays)
    high, low = high.astype(f32), low.astype(f32)
    tail = iota((8, inputs.shape[1]), 0)
    for k in range(blocks):
        at = slice(k * LANES, (k + 1) * LANES)
        left = pushes(proj_rows[:state_count, at], to_end, width, narrow[at], k, head_count)
        for g in range(groups):
            r = k * groups + g
            payload[r, :state_count, :] = left[g].astype(bf16)
            payload[r, state_count:, :] = jnp.where(
                tail == 0, high[r : r + 1], jnp.where(tail == 1, low[r : r + 1], 0.0)
            ).astype(bf16)


def spread(row, lanes):
    return dot(jnp.broadcast_to(row, (8, row.shape[-1])), lanes, highest)[:1]


def make_within(group):
    def body(values, proj, b_rows, run_col, less_row, skips, outputs):
        head_count = skips.shape[-1]
        count, width_all = values.shape
        skip = spread(skips[...], head_lanes(head_count, width_all // head_count))
        for k in range(count // LANES):
            at = slice(k * LANES, (k + 1) * LANES)
            block = values[at, :]
            own = within(
                proj[at, :], b_rows[:, at], group, run_col[...], less_row[...], block, k, head_count
            )
            outputs[at, :] = own + skip * block.astype(f32)

    return body


def enter(payload, entering):
    device_count, _, width_all = payload.shape
    state_count = entering.shape[1]
    state = jnp.zeros((state_count, width_all), f32)
    for k in range(device_count):
        entering[k] = state.astype(bf16)
        tail = payload[k, state_count:, :].astype(f32)
        decay = tail[0:1] + tail[1:2]
        state = decay * state + payload[k, :state_count, :].astype(f32)


def reach_lanes(run_col_block, block, head_count, width_all):
    shape = (run_col_block.shape[1], width_all)
    row, lane = iota(shape, 0), iota(shape, 1)
    here = (row // head_count == block) & (row % head_count == lane // (width_all // head_count))
    lanes = jnp.where(here, 1.0, 0.0).astype(bf16)
    high, low = halves(jnp.exp(run_col_block))
    return dot(high, lanes) + dot(low, lanes)


def normed(values, gain):
    square = jnp.mean(values * values, axis=-1, keepdims=True)
    return values * lax.rsqrt(square + 1e-05) * gain


def swap_matrix(count, inner):
    outer = count // inner
    place, source = iota((count, count), 0), iota((count, count), 1)
    return jnp.where((place % outer) * inner + place // outer == source, 1.0, 0.0).astype(bf16)


def finish_rows(outputs, proj, run_col, entering, gain, lines):
    line_count, state_count, width_all = entering.shape
    count = outputs.shape[0]
    width = count // line_count
    head_count = proj.shape[1] - 2 * state_count
    done = []
    for k in range(count // LANES):
        at = slice(k * LANES, (k + 1) * LANES)
        reach = reach_lanes(run_col[...], k, head_count, width_all)
        extra = []
        for r in range(k * LANES // width, (k + 1) * LANES // width):
            high, low = halves(proj[r * width : (r + 1) * width, :])
            state = jnp.concatenate(
                [
                    jnp.zeros((state_count, width_all), bf16),
                    entering[r],
                    jnp.zeros((head_count, width_all), bf16),
                ],
                axis=0,
            )
            extra.append(dot(high, state) + dot(low, state))
        whole = outputs[at, :] + jnp.concatenate(extra, axis=0) * reach
        done.append(normed(whole, gain[...]).astype(bf16))
    lines[...] = dot(swap_matrix(count, width), jnp.concatenate(done, axis=0)).astype(bf16)


def scan_columns(lines, w_proj, bias, rates, skips, outputs):
    count, width_all = lines.shape
    head_count = bias.shape[-1]
    inputs = lines[...]
    proj = dot(inputs, w_proj[...])
    proj_rows = lax.dot_general(
        w_proj[...], inputs, (((0,), (1,)), ((), ())), preferred_element_type=f32
    )
    state_count = (proj.shape[1] - head_count) // 2
    running, less, totals = step_terms(proj_rows, bias[...], rates[...], LANES)
    run_col = jnp.transpose(running)
    to_end = jnp.exp(totals - less)
    total_cols = jnp.transpose(totals)
    lanes = head_lanes(head_count, width_all // head_count)
    skip = spread(skips[...], lanes)
    blocks = count // LANES
    shape = (8, blocks * head_count)
    here = iota(shape, 1) // head_count == iota(shape, 0)
    picked = jnp.where(here, jnp.broadcast_to(total_cols[:1], shape), 0.0)
    decays = jnp.exp(dot(picked, jnp.concatenate([lanes] * blocks, axis=0), highest))
    state = jnp.zeros((state_count, width_all), f32)
    for k in range(blocks):
        at = slice(k * LANES, (k + 1) * LANES)
        block = inputs[at]
        b_block = proj_rows[:state_count, at]
        own = within(proj[at], b_block, LANES, run_col, less, block, k, head_count)
        own = own + skip * block.astype(f32)
        if k > 0:
            padded = jnp.concatenate(
                [
                    jnp.zeros((state_count, width_all), f32),
                    state,
                    jnp.zeros((head_count, width_all), f32),
                ],
                axis=0,
            )
            own = own + dot(proj[at], padded, highest) * reach_lanes(
                run_col, k, head_count, width_all
            )
        outputs[at, :] = own.astype(bf16)
        if k + 1 < blocks:
            left = pushes(b_block, to_end, LANES, block, k, head_count)[0]
            state = decays[k : k + 1] * state + left


def make_gate(width):
    def gate(masked, w_gate, gates):
        value = dot(masked[...], w_gate[...])
        gates[...] = value / (1.0 + jnp.exp(-value))

    return gate


def make_finish(width):
    def finish(columns, gates, masked, w_out, gain, mixed):
        count = columns.shape[0]
        swapped = dot(swap_matrix(count, count // width), columns[...])
        act = (normed(swapped, gain[...]) * gates[...]).astype(bf16)
        mixed[...] = (masked[...].astype(f32) + dot(act, w_out[...])).astype(bf16)

    return finish


def call(body, out_shape, *args, flops=0, name=None):
    in_place = pl.BlockSpec(memory_space=pltpu.VMEM)
    single = not isinstance(out_shape, tuple)
    return pl.pallas_call(
        body,
        out_shape=out_shape,
        in_specs=[in_place] * len(args),
        out_specs=in_place if single else tuple(in_place for _ in out_shape),
        name=name,
        cost_estimate=pl.CostEstimate(flops=flops, bytes_accessed=4 << 20, transcendentals=0),
        compiler_params=pltpu.CompilerParams(vmem_limit_bytes=24 << 20),
    )(*args)


def on_device(
    patches,
    tissue,
    w_value,
    w_across,
    w_down,
    w_gate,
    w_out,
    step_bias_across,
    step_bias_down,
    rates_across,
    rates_down,
    skip_across,
    skip_down,
    gain_across,
    gain_final,
):
    shape = jax.ShapeDtypeStruct
    line_count, width, width_all = patches.shape
    count = line_count * width
    head_count = rates_across.shape[0]
    proj_count = w_across.shape[1]
    state_count = (proj_count - head_count) // 2
    blocks = count // LANES
    row = lambda x: x.reshape(1, -1)
    masked, values, proj, b_rows, run_col, less_row, payload = call(
        prepare,
        (
            shape((count, width_all), bf16),
            shape((count, width_all), bf16),
            shape((count, proj_count), f32),
            shape((state_count, count), f32),
            shape((LANES, blocks * head_count), f32),
            shape((blocks * head_count, LANES), f32),
            shape((line_count, state_count + 8, width_all), bf16),
        ),
        patches.reshape(count, width_all),
        tissue,
        w_value,
        w_across,
        row(step_bias_across),
        row(rates_across),
        flops=5 * 10**8,
        name="prepare",
    )
    payload = lax.all_to_all(payload, "cols", 0, 0, tiled=True)
    entering = call(
        enter,
        shape((payload.shape[0], state_count, width_all), bf16),
        payload,
        flops=10**6,
        name="enter",
    )
    entering = lax.all_to_all(entering, "cols", 0, 0, tiled=True)
    outputs = call(
        make_within(width),
        shape((count, width_all), f32),
        values,
        proj,
        b_rows,
        run_col,
        less_row,
        row(skip_across),
        flops=10**9,
        name="within_rows",
    )
    gates = call(
        make_gate(width),
        shape((count, width_all), f32),
        masked,
        w_gate,
        flops=5 * 10**8,
        name="gate",
    )
    lines = call(
        finish_rows,
        shape((count, width_all), bf16),
        outputs,
        proj,
        run_col,
        entering,
        row(gain_across),
        flops=5 * 10**8,
        name="finish_rows",
    )
    split = (count // line_count, line_count, width_all)
    lines = lax.all_to_all(lines.reshape(split), "rows", 0, 0, tiled=True)
    columns = call(
        scan_columns,
        shape((count, width_all), bf16),
        lines.reshape(count, width_all),
        w_down,
        row(step_bias_down),
        row(rates_down),
        row(skip_down),
        flops=10**9,
        name="scan_columns",
    )
    columns = lax.all_to_all(columns.reshape(split), "rows", 0, 0, tiled=True)
    mixed = call(
        make_finish(width),
        shape((count, width_all), bf16),
        columns.reshape(count, width_all),
        gates,
        masked,
        w_out,
        row(gain_final),
        flops=5 * 10**8,
        name="finish",
    )
    return mixed.reshape(patches.shape)


def solution(mesh):
    return jax.shard_map(
        on_device,
        mesh=mesh,
        in_specs=(P("rows", "cols", None), P("rows", "cols")) + (P(),) * 13,
        out_specs=P("rows", "cols", None),
        check_vma=False,
    )
```

```python
import jax
import jax.numpy as jnp
from jax import lax
from jax.experimental import pallas as pl
from jax.experimental.pallas import tpu as pltpu
from jax.sharding import PartitionSpec as P

bf16, f32 = jnp.bfloat16, jnp.float32
LANES = 128
CAP = 80.0


def iota(shape, dim):
    return lax.broadcasted_iota(jnp.int32, shape, dim)


def dot(a, b):
    return jnp.dot(a, b, preferred_element_type=f32)


def dot_t(a, b):
    return lax.dot_general(a, b, (((1,), (1,)), ((), ())), preferred_element_type=f32)


def halves(x):
    high = x.astype(bf16)
    return high, (x - high.astype(f32)).astype(bf16)


def softplus(v):
    return jnp.maximum(v, 0.0) + jnp.log1p(jnp.exp(-jnp.abs(v)))


def dot3(a, b):
    (ah, al), (bh, bl) = halves(a), halves(b)
    return dot(ah, bh) + (dot(al, bh) + dot(ah, bl))


def by_ones(a, ones):
    high, rest = a.astype(bf16), None
    rest = a - high.astype(f32)
    middle = rest.astype(bf16)
    low = (rest - middle.astype(f32)).astype(bf16)
    n = a.shape[0]
    whole = dot(jnp.concatenate([high.astype(f32), middle.astype(f32), low.astype(f32)], axis=0).astype(bf16), ones)
    return whole[:n] + (whole[n : 2 * n] + whole[2 * n :])


def as_column(row):
    n = row.shape[-1]
    square = jnp.broadcast_to(row, (n, n))
    return jnp.sum(jnp.where(iota((n, n), 0) == iota((n, n), 1), square, 0.0), axis=1, keepdims=True)


def head_lanes(head_count, width):
    shape = (head_count, head_count * width)
    return jnp.where(iota(shape, 1) // width == iota(shape, 0), 1.0, 0.0)


def step_terms(proj_rows, bias, rates, group):
    head_count = bias.shape[-1]
    steps = softplus(proj_rows[-head_count:] + as_column(bias))
    falls = -steps * as_column(rates)
    logs = jnp.log(steps)
    blocks = proj_rows.shape[1] // LANES
    stack = lambda x: jnp.concatenate([x[:, k * LANES : (k + 1) * LANES] for k in range(blocks)], axis=0)
    falls, logs = stack(falls), stack(logs)
    source, target = iota((LANES, LANES), 0), iota((LANES, LANES), 1)
    same = source // group == target // group
    running = by_ones(falls, jnp.where(same & (source <= target), 1.0, 0.0).astype(bf16))
    totals = by_ones(falls, jnp.where(same, 1.0, 0.0).astype(bf16))
    return running, running - logs, totals


def products(proj_block, b_block):
    state_count = b_block.shape[0]
    rest = proj_block.shape[1] - 2 * state_count
    padded = jnp.concatenate(
        [jnp.zeros_like(b_block), b_block, jnp.zeros((rest, b_block.shape[1]), f32)], axis=0
    )
    return dot3(proj_block, padded)


def within(proj_block, b_block, group, run_col, less_row, values, block, head_count):
    source, target = iota((LANES, LANES), 1), iota((LANES, LANES), 0)
    keep = (source // group == target // group) & (source <= target)
    inter = jnp.where(keep, products(proj_block, b_block), 0.0)
    low_lanes = iota((LANES, LANES), 1) < LANES // 2
    tiles = []
    for pair in range(head_count // 2):
        weights = []
        for head in (2 * pair, 2 * pair + 1):
            at = block * head_count + head
            spans = run_col[:, at : at + 1] - less_row[at : at + 1, :]
            weights.append((jnp.exp(jnp.minimum(spans, CAP)) * inter).astype(bf16))
        both = dot(jnp.concatenate(weights, axis=0), values[:, pair * LANES : (pair + 1) * LANES])
        tiles.append(jnp.where(low_lanes, both[:LANES], both[LANES:]))
    return jnp.concatenate(tiles, axis=1)


def pushes(b_block, to_end, group, values, block, head_count):
    state_count = b_block.shape[0]
    groups = LANES // group
    lane = iota((state_count, LANES), 1)
    tiles = [[] for _ in range(groups)]
    for pair in range(head_count // 2):
        rows = []
        for g in range(groups):
            for head in (2 * pair, 2 * pair + 1):
                at = block * head_count + head
                coef = b_block * to_end[at : at + 1, :]
                rows.append(jnp.where(lane // group == g, coef, 0.0).astype(bf16))
        left = dot(jnp.concatenate(rows, axis=0), values[:, pair * LANES : (pair + 1) * LANES])
        for g in range(groups):
            top = left[2 * g * state_count : (2 * g + 1) * state_count]
            bottom = left[(2 * g + 1) * state_count : (2 * g + 2) * state_count]
            tiles[g].append(jnp.where(lane < LANES // 2, top, bottom))
    return [jnp.concatenate(t, axis=1) for t in tiles]


def fetch(sources, targets, sems):
    copies = [
        pltpu.make_async_copy(source, target, sems.at[i])
        for i, (source, target) in enumerate(zip(sources, targets))
    ]
    for copy in copies:
        copy.start()
    return copies


def prepare(*refs):
    patches, tissue, w_value, w_proj, bias, rates = refs[:6]
    masked, values, proj, b_rows, run_col, less_row, payload = refs[6:13]
    patches_in, tissue_in, value_in, proj_in, bias_in, rates_in, sems = refs[13:]
    copies = fetch(
        (tissue, patches, w_proj, bias, rates, w_value),
        (tissue_in, patches_in, proj_in, bias_in, rates_in, value_in),
        sems,
    )
    line_count, width = tissue_in.shape
    head_count = bias_in.shape[-1]
    copies[0].wait()
    flags = jnp.transpose(tissue_in[...].astype(f32))
    copies[1].wait()
    for r in range(line_count):
        keep = jnp.broadcast_to(flags[:, r : r + 1], (width, patches_in.shape[1])).astype(bf16)
        rows = slice(r * width, (r + 1) * width)
        masked[rows, :] = patches_in[rows, :] * keep
    inputs = masked[...]
    for copy in copies[2:5]:
        copy.wait()
    proj[...] = dot_t(inputs, proj_in[...])
    proj_rows = dot_t(proj_in[...], inputs)
    state_count = (proj.shape[1] - head_count) // 2
    b_rows[...] = proj_rows[:state_count]
    running, less, totals = step_terms(proj_rows, bias_in[...], rates_in[...], width)
    less_row[...] = less
    run_col[...] = jnp.transpose(running)
    to_end = jnp.exp(totals - less)
    total_cols = jnp.transpose(totals)
    blocks = inputs.shape[0] // LANES
    groups = LANES // width
    shape = (line_count, blocks * head_count)
    line, column = iota(shape, 0), iota(shape, 1)
    picked = jnp.zeros(shape, f32)
    for g in range(groups):
        here = (line % groups == g) & (column // head_count == line // groups)
        picked = jnp.where(here, total_cols[g * width : g * width + 1, :], picked)
    lanes = jnp.concatenate([head_lanes(head_count, inputs.shape[1] // head_count)] * blocks, axis=0)
    decays = jnp.exp(by_ones(picked, lanes.astype(bf16)))
    keep_decays(payload, decays)
    copies[5].wait()
    narrow = dot(inputs, value_in[...]).astype(bf16)
    values[...] = narrow
    for k in range(blocks):
        at = slice(k * LANES, (k + 1) * LANES)
        left = pushes(proj_rows[:state_count, at], to_end, width, narrow[at], k, head_count)
        for g in range(groups):
            r = k * groups + g
            payload[r * state_count : (r + 1) * state_count, :] = left[g].astype(bf16)


def keep_decays(payload, decays):
    high, low = halves(decays)
    pair = jnp.concatenate([high.astype(f32), low.astype(f32)], axis=0).astype(bf16)
    payload[payload.shape[0] - pair.shape[0] :, :] = pair


def read_decays(payload, line_count):
    pair = payload[payload.shape[0] - 2 * line_count :, :].astype(f32)
    return pair[:line_count] + pair[line_count:]


def line_rows(r, state_count):
    return slice(r * state_count, (r + 1) * state_count)


def first_step(own, came, state, span, sent):
    line_count = span.shape[0]
    state_count = state.shape[0] // line_count
    decays, before = read_decays(own, line_count), read_decays(came, line_count)
    span[...] = before
    keep_decays(sent, decays * before)
    for r in range(line_count):
        at = line_rows(r, state_count)
        entered = came[at, :].astype(f32)
        state[at, :] = entered
        sent[at, :] = (own[at, :].astype(f32) + decays[r : r + 1] * entered).astype(bf16)


def second_step(own, came, state, span, states, spans, sent):
    line_count = span.shape[0]
    state_count = state.shape[0] // line_count
    decays, before = read_decays(own, line_count), read_decays(came, line_count)
    over = span[...]
    spans[...] = over * before
    for r in range(line_count):
        at = line_rows(r, state_count)
        entered = state[at, :] + over[r : r + 1] * came[at, :].astype(f32)
        states[at, :] = entered
        sent[at, :] = (own[at, :].astype(f32) + decays[r : r + 1] * entered).astype(bf16)


def spread(row, lanes):
    return by_ones(jnp.broadcast_to(row, (8, row.shape[-1])), lanes.astype(bf16))[:1]


def make_within(group):
    def body(values, proj, b_rows, run_col, less_row, skips, *refs):
        given, (outputs, reach), passed = refs[:5], refs[5:7], refs[7:]
        for source, target in zip(given, passed):
            target[...] = source[...]
        head_count = skips.shape[-1]
        count, width_all = values.shape
        skip = spread(skips[...], head_lanes(head_count, width_all // head_count))
        for k in range(count // LANES):
            at = slice(k * LANES, (k + 1) * LANES)
            block = values[at, :]
            own = within(
                proj[at, :], b_rows[:, at], group, run_col[...], less_row[...], block, k, head_count
            )
            outputs[at, :] = own + skip * block.astype(f32)
            reach[at, :] = reach_lanes(run_col[...], k, head_count, width_all)

    return body


def reach_lanes(run_col_block, block, head_count, width_all):
    shape = (run_col_block.shape[1], width_all)
    row, lane = iota(shape, 0), iota(shape, 1)
    here = (row // head_count == block) & (row % head_count == lane // (width_all // head_count))
    lanes = jnp.where(here, 1.0, 0.0).astype(bf16)
    high, low = halves(jnp.exp(run_col_block))
    return dot(high, lanes) + dot(low, lanes)


def normed(values, gain):
    square = jnp.mean(values * values, axis=-1, keepdims=True)
    return values * lax.rsqrt(square + 1e-05) * gain


def swap_matrix(count, inner):
    outer = count // inner
    place, source = iota((count, count), 0), iota((count, count), 1)
    return jnp.where((place % outer) * inner + place // outer == source, 1.0, 0.0).astype(bf16)


def finish_rows(outputs, reach, proj, states, spans, came, gain, swap, lines):
    line_count, width_all = spans.shape
    state_count = states.shape[0] // line_count
    count = outputs.shape[0]
    width = count // line_count
    head_count = proj.shape[1] - 2 * state_count
    done = []
    for r in range(line_count):
        at = line_rows(r, state_count)
        state = states[at, :] + spans[r : r + 1, :] * came[at, :].astype(f32)
        padded = jnp.concatenate(
            [
                jnp.zeros((state_count, width_all), f32),
                state,
                jnp.zeros((head_count, width_all), f32),
            ],
            axis=0,
        )
        rows = slice(r * width, (r + 1) * width)
        whole = outputs[rows, :] + dot3(proj[rows, :], padded) * reach[rows, :]
        done.append(normed(whole, gain[...]).astype(bf16))
    lines[...] = dot(swap[...], jnp.concatenate(done, axis=0)).astype(bf16)


def scan_columns(lines, w_proj, bias, rates, skips, outputs):
    count, width_all = lines.shape
    head_count = bias.shape[-1]
    inputs = lines[...]
    proj = dot_t(inputs, w_proj[...])
    proj_rows = dot_t(w_proj[...], inputs)
    state_count = (proj.shape[1] - head_count) // 2
    running, less, totals = step_terms(proj_rows, bias[...], rates[...], LANES)
    run_col = jnp.transpose(running)
    to_end = jnp.exp(totals - less)
    total_cols = jnp.transpose(totals)
    lanes = head_lanes(head_count, width_all // head_count)
    skip = spread(skips[...], lanes)
    blocks = count // LANES
    shape = (8, blocks * head_count)
    here = iota(shape, 1) // head_count == iota(shape, 0)
    picked = jnp.where(here, jnp.broadcast_to(total_cols[:1], shape), 0.0)
    decays = jnp.exp(by_ones(picked, jnp.concatenate([lanes] * blocks, axis=0).astype(bf16)))
    state = jnp.zeros((state_count, width_all), f32)
    for k in range(blocks):
        at = slice(k * LANES, (k + 1) * LANES)
        block = inputs[at]
        b_block = proj_rows[:state_count, at]
        own = within(proj[at], b_block, LANES, run_col, less, block, k, head_count)
        own = own + skip * block.astype(f32)
        if k > 0:
            padded = jnp.concatenate(
                [
                    jnp.zeros((state_count, width_all), f32),
                    state,
                    jnp.zeros((head_count, width_all), f32),
                ],
                axis=0,
            )
            own = own + dot3(proj[at], padded) * reach_lanes(
                run_col, k, head_count, width_all
            )
        outputs[at, :] = own.astype(bf16)
        if k + 1 < blocks:
            left = pushes(b_block, to_end, LANES, block, k, head_count)[0]
            state = decays[k : k + 1] * state + left


def make_gate(width):
    def gate(masked, w_gate, gates, swap, back):
        value = dot(masked[...], w_gate[...])
        gates[...] = value / (1.0 + jnp.exp(-value))
        count = masked.shape[0]
        swap[...] = swap_matrix(count, width)
        back[...] = swap_matrix(count, count // width)

    return gate


def finish(columns, gates, masked, w_out, gain, back, mixed, rows_out, sems):
    act = (normed(dot(back[...], columns[...]), gain[...]) * gates[...]).astype(bf16)
    copies = []
    part = mixed.shape[1] // sems.shape[0]
    for k in range(sems.shape[0]):
        at = slice(k * part, (k + 1) * part)
        rows_out[:, at] = (masked[:, at].astype(f32) + dot(act, w_out[:, at])).astype(bf16)
        copies.append(pltpu.make_async_copy(rows_out.at[:, at], mixed.at[:, at], sems.at[k]))
        copies[-1].start()
    for copy in copies:
        copy.wait()


def shifted(value, axis, by):
    count = lax.axis_size(axis)
    return lax.ppermute(value, axis, [(i, i + by) for i in range(count - by)])


IN_VMEM = pl.BlockSpec(memory_space=pltpu.VMEM)
IN_PLACE = pl.BlockSpec(memory_space=pltpu.HBM)


def call(body, out_shape, *args, flops=0, name=None, ins=IN_VMEM, outs=IN_VMEM, scratch=()):
    single = not isinstance(out_shape, tuple)
    return pl.pallas_call(
        body,
        out_shape=out_shape,
        in_specs=[ins] * len(args),
        out_specs=outs if single else tuple(outs for _ in out_shape),
        scratch_shapes=scratch,
        name=name,
        cost_estimate=pl.CostEstimate(flops=flops, bytes_accessed=4 << 20, transcendentals=0),
        compiler_params=pltpu.CompilerParams(vmem_limit_bytes=24 << 20),
    )(*args)


def on_device(
    patches,
    tissue,
    w_value,
    w_across,
    w_down,
    w_gate,
    w_out,
    step_bias_across,
    step_bias_down,
    rates_across,
    rates_down,
    skip_across,
    skip_down,
    gain_across,
    gain_final,
):
    shape = jax.ShapeDtypeStruct
    line_count, width, width_all = patches.shape
    count = line_count * width
    head_count = rates_across.shape[0]
    proj_count = w_across.shape[1]
    state_count = (proj_count - head_count) // 2
    blocks = count // LANES
    row = lambda x: x.reshape(1, -1)
    state_rows = line_count * state_count
    given = (
        patches.reshape(count, width_all),
        tissue,
        w_value,
        w_across.T,
        row(step_bias_across),
        row(rates_across),
    )
    masked, values, proj, b_rows, run_col, less_row, payload = call(
        prepare,
        (
            shape((count, width_all), bf16),
            shape((count, width_all), bf16),
            shape((count, proj_count), f32),
            shape((state_count, count), f32),
            shape((LANES, blocks * head_count), f32),
            shape((blocks * head_count, LANES), f32),
            shape((state_rows + 2 * line_count, width_all), bf16),
        ),
        *(pltpu.with_memory_space_constraint(x, pltpu.HBM) for x in given),
        flops=5 * 10**8,
        name="prepare",
        ins=IN_PLACE,
        scratch=[pltpu.VMEM(x.shape, x.dtype) for x in given]
        + [pltpu.SemaphoreType.DMA((len(given),))],
    )
    came = shifted(payload, "cols", 1)
    state, span, sent = call(
        first_step,
        (
            shape((state_rows, width_all), f32),
            shape((line_count, width_all), f32),
            shape(payload.shape, bf16),
        ),
        payload,
        came,
        flops=10**6,
        name="first_step",
    )
    came = shifted(sent, "cols", 2)
    early, _ = lax.optimization_barrier((masked, sent))
    gates, swap, back = call(
        make_gate(width),
        (
            shape((count, width_all), f32),
            shape((count, count), bf16),
            shape((count, count), bf16),
        ),
        early,
        w_gate,
        flops=5 * 10**8,
        name="gate",
    )
    came, gates = lax.optimization_barrier((came, gates))
    states, spans, sent = call(
        second_step,
        (
            shape((state_rows, width_all), f32),
            shape((line_count, width_all), f32),
            shape((state_rows, width_all), bf16),
        ),
        payload,
        came,
        state,
        span,
        flops=10**6,
        name="second_step",
    )
    came = shifted(sent, "cols", 4)
    values, _ = lax.optimization_barrier((values, sent))
    passed = tuple(
        row(x) for x in (step_bias_down, rates_down, skip_down, gain_across, gain_final)
    )
    outputs, reach, bias_down, rate_down, skips_down, gains_across, gains_final = call(
        make_within(width),
        (shape((count, width_all), f32), shape((count, width_all), f32))
        + tuple(shape(x.shape, x.dtype) for x in passed),
        values,
        proj,
        b_rows,
        run_col,
        less_row,
        row(skip_across),
        *passed,
        flops=10**9,
        name="within_rows",
    )
    lines = call(
        finish_rows,
        shape((count, width_all), bf16),
        outputs,
        reach,
        proj,
        states,
        spans,
        came,
        gains_across,
        swap,
        flops=5 * 10**8,
        name="finish_rows",
    )
    split = (count // line_count, line_count, width_all)
    lines = lax.all_to_all(lines.reshape(split), "rows", 0, 0, tiled=True)
    columns = call(
        scan_columns,
        shape((count, width_all), bf16),
        lines.reshape(count, width_all),
        w_down.T,
        bias_down,
        rate_down,
        skips_down,
        flops=10**9,
        name="scan_columns",
    )
    columns = lax.all_to_all(columns.reshape(split), "rows", 0, 0, tiled=True)
    mixed = call(
        finish,
        shape((count, width_all), bf16),
        columns.reshape(count, width_all),
        gates,
        masked,
        w_out,
        gains_final,
        back,
        flops=5 * 10**8,
        name="finish",
        outs=IN_PLACE,
        scratch=[
            pltpu.VMEM((count, width_all), bf16),
            pltpu.SemaphoreType.DMA((2,)),
        ],
    )
    return mixed.reshape(patches.shape)


def solution(mesh):
    return jax.shard_map(
        on_device,
        mesh=mesh,
        in_specs=(P("rows", "cols", None), P("rows", "cols")) + (P(),) * 13,
        out_specs=P("rows", "cols", None),
        check_vma=False,
    )
```

```python
import functools

import jax
import jax.numpy as jnp
from jax import lax
from jax.experimental import pallas as pl
from jax.experimental.pallas import tpu as pltpu
from jax.sharding import PartitionSpec as P

bf16, f32 = jnp.bfloat16, jnp.float32
LANES = 128
CAP = 80.0
FIRST_DOWN = 46
FIRST_BACK = 46


def iota(shape, dim):
    return lax.broadcasted_iota(jnp.int32, shape, dim)


def dot(a, b):
    return jnp.dot(a, b, preferred_element_type=f32)


def dot_t(a, b):
    return lax.dot_general(a, b, (((1,), (1,)), ((), ())), preferred_element_type=f32)


def halves(x):
    high = x.astype(bf16)
    return high, (x - high.astype(f32)).astype(bf16)


def softplus(v):
    return jnp.maximum(v, 0.0) + jnp.log1p(jnp.exp(-jnp.abs(v)))


def dot3(a, b):
    (ah, al), (bh, bl) = halves(a), halves(b)
    return dot(ah, bh) + (dot(al, bh) + dot(ah, bl))


def by_ones(a, ones):
    high, rest = a.astype(bf16), None
    rest = a - high.astype(f32)
    middle = rest.astype(bf16)
    low = (rest - middle.astype(f32)).astype(bf16)
    n = a.shape[0]
    whole = dot(jnp.concatenate([high.astype(f32), middle.astype(f32), low.astype(f32)], axis=0).astype(bf16), ones)
    return whole[:n] + (whole[n : 2 * n] + whole[2 * n :])


def as_column(row):
    n = row.shape[-1]
    square = jnp.broadcast_to(row, (n, n))
    return jnp.sum(jnp.where(iota((n, n), 0) == iota((n, n), 1), square, 0.0), axis=1, keepdims=True)


def head_lanes(head_count, width):
    shape = (head_count, head_count * width)
    return jnp.where(iota(shape, 1) // width == iota(shape, 0), 1.0, 0.0)


def step_terms(proj_rows, bias, rates, group):
    head_count = bias.shape[-1]
    steps = softplus(proj_rows[-head_count:] + as_column(bias))
    falls = -steps * as_column(rates)
    logs = jnp.log(steps)
    blocks = proj_rows.shape[1] // LANES
    stack = lambda x: jnp.concatenate([x[:, k * LANES : (k + 1) * LANES] for k in range(blocks)], axis=0)
    falls, logs = stack(falls), stack(logs)
    source, target = iota((LANES, LANES), 0), iota((LANES, LANES), 1)
    same = source // group == target // group
    running = by_ones(falls, jnp.where(same & (source <= target), 1.0, 0.0).astype(bf16))
    totals = by_ones(falls, jnp.where(same, 1.0, 0.0).astype(bf16))
    return running, running - logs, totals


def products(proj_block, b_block):
    state_count = b_block.shape[0]
    rest = proj_block.shape[1] - 2 * state_count
    padded = jnp.concatenate(
        [jnp.zeros_like(b_block), b_block, jnp.zeros((rest, b_block.shape[1]), f32)], axis=0
    )
    return dot3(proj_block, padded)


def within(proj_block, b_block, group, run_col, less_row, values, block, head_count):
    source, target = iota((LANES, LANES), 1), iota((LANES, LANES), 0)
    keep = (source // group == target // group) & (source <= target)
    inter = jnp.where(keep, products(proj_block, b_block), 0.0)
    low_lanes = iota((LANES, LANES), 1) < LANES // 2
    tiles = []
    for pair in range(head_count // 2):
        weights = []
        for head in (2 * pair, 2 * pair + 1):
            at = block * head_count + head
            spans = run_col[:, at : at + 1] - less_row[at : at + 1, :]
            weights.append((jnp.exp(jnp.minimum(spans, CAP)) * inter).astype(bf16))
        both = dot(jnp.concatenate(weights, axis=0), values[:, pair * LANES : (pair + 1) * LANES])
        tiles.append(jnp.where(low_lanes, both[:LANES], both[LANES:]))
    return jnp.concatenate(tiles, axis=1)


def pushes(b_block, to_end, group, values, block, head_count):
    state_count = b_block.shape[0]
    groups = LANES // group
    lane = iota((state_count, LANES), 1)
    tiles = [[] for _ in range(groups)]
    for pair in range(head_count // 2):
        rows = []
        for g in range(groups):
            for head in (2 * pair, 2 * pair + 1):
                at = block * head_count + head
                coef = b_block * to_end[at : at + 1, :]
                rows.append(jnp.where(lane // group == g, coef, 0.0).astype(bf16))
        left = dot(jnp.concatenate(rows, axis=0), values[:, pair * LANES : (pair + 1) * LANES])
        for g in range(groups):
            top = left[2 * g * state_count : (2 * g + 1) * state_count]
            bottom = left[(2 * g + 1) * state_count : (2 * g + 2) * state_count]
            tiles[g].append(jnp.where(lane < LANES // 2, top, bottom))
    return [jnp.concatenate(t, axis=1) for t in tiles]


def fetch(sources, targets, sems):
    copies = [
        pltpu.make_async_copy(source, target, sems.at[i])
        for i, (source, target) in enumerate(zip(sources, targets))
    ]
    for copy in copies:
        copy.start()
    return copies


def prepare(*refs):
    patches, tissue, w_value, w_proj, bias, rates = refs[:6]
    masked, values, proj, b_rows, run_col, less_row, payload = refs[6:13]
    patches_in, tissue_in, value_in, proj_in, bias_in, rates_in, sems = refs[13:]
    copies = fetch(
        (tissue, patches, w_proj, bias, rates, w_value),
        (tissue_in, patches_in, proj_in, bias_in, rates_in, value_in),
        sems,
    )
    line_count, width = tissue_in.shape
    head_count = bias_in.shape[-1]
    copies[0].wait()
    flags = jnp.transpose(tissue_in[...].astype(f32))
    copies[1].wait()
    for r in range(line_count):
        keep = jnp.broadcast_to(flags[:, r : r + 1], (width, patches_in.shape[1])).astype(bf16)
        rows = slice(r * width, (r + 1) * width)
        masked[rows, :] = patches_in[rows, :] * keep
    inputs = masked[...]
    for copy in copies[2:5]:
        copy.wait()
    proj[...] = dot_t(inputs, proj_in[...])
    proj_rows = dot_t(proj_in[...], inputs)
    state_count = (proj.shape[1] - head_count) // 2
    b_rows[...] = proj_rows[:state_count]
    running, less, totals = step_terms(proj_rows, bias_in[...], rates_in[...], width)
    less_row[...] = less
    run_col[...] = jnp.transpose(running)
    to_end = jnp.exp(totals - less)
    total_cols = jnp.transpose(totals)
    blocks = inputs.shape[0] // LANES
    groups = LANES // width
    shape = (line_count, blocks * head_count)
    line, column = iota(shape, 0), iota(shape, 1)
    picked = jnp.zeros(shape, f32)
    for g in range(groups):
        here = (line % groups == g) & (column // head_count == line // groups)
        picked = jnp.where(here, total_cols[g * width : g * width + 1, :], picked)
    lanes = jnp.concatenate([head_lanes(head_count, inputs.shape[1] // head_count)] * blocks, axis=0)
    decays = jnp.exp(by_ones(picked, lanes.astype(bf16)))
    keep_decays(payload, decays)
    copies[5].wait()
    narrow = dot(inputs, value_in[...]).astype(bf16)
    values[...] = narrow
    for k in range(blocks):
        at = slice(k * LANES, (k + 1) * LANES)
        left = pushes(proj_rows[:state_count, at], to_end, width, narrow[at], k, head_count)
        for g in range(groups):
            r = k * groups + g
            payload[r * state_count : (r + 1) * state_count, :] = left[g].astype(bf16)


def keep_decays(payload, decays):
    high, low = halves(decays)
    pair = jnp.concatenate([high.astype(f32), low.astype(f32)], axis=0).astype(bf16)
    payload[payload.shape[0] - pair.shape[0] :, :] = pair


def read_decays(payload, line_count):
    pair = payload[payload.shape[0] - 2 * line_count :, :].astype(f32)
    return pair[:line_count] + pair[line_count:]


def line_rows(r, state_count):
    return slice(r * state_count, (r + 1) * state_count)


def first_step(own, came, state, span, sent):
    line_count = span.shape[0]
    state_count = state.shape[0] // line_count
    decays, before = read_decays(own, line_count), read_decays(came, line_count)
    span[...] = before
    keep_decays(sent, decays * before)
    for r in range(line_count):
        at = line_rows(r, state_count)
        entered = came[at, :].astype(f32)
        state[at, :] = entered
        sent[at, :] = (own[at, :].astype(f32) + decays[r : r + 1] * entered).astype(bf16)


def second_step(own, came, state, span, states, spans, sent):
    line_count = span.shape[0]
    state_count = state.shape[0] // line_count
    decays, before = read_decays(own, line_count), read_decays(came, line_count)
    over = span[...]
    spans[...] = over * before
    for r in range(line_count):
        at = line_rows(r, state_count)
        entered = state[at, :] + over[r : r + 1] * came[at, :].astype(f32)
        states[at, :] = entered
        sent[at, :] = (own[at, :].astype(f32) + decays[r : r + 1] * entered).astype(bf16)


def spread(row, lanes):
    return by_ones(jnp.broadcast_to(row, (8, row.shape[-1])), lanes.astype(bf16))[:1]


def make_within(group):
    def body(values, proj, b_rows, run_col, less_row, skips, *refs):
        given, (outputs, reach), passed = refs[:5], refs[5:7], refs[7:]
        for source, target in zip(given, passed):
            target[...] = source[...]
        head_count = skips.shape[-1]
        count, width_all = values.shape
        skip = spread(skips[...], head_lanes(head_count, width_all // head_count))
        for k in range(count // LANES):
            at = slice(k * LANES, (k + 1) * LANES)
            block = values[at, :]
            own = within(
                proj[at, :], b_rows[:, at], group, run_col[...], less_row[...], block, k, head_count
            )
            outputs[at, :] = own + skip * block.astype(f32)
            reach[at, :] = reach_lanes(run_col[...], k, head_count, width_all)

    return body


def reach_lanes(run_col_block, block, head_count, width_all):
    shape = (run_col_block.shape[1], width_all)
    row, lane = iota(shape, 0), iota(shape, 1)
    here = (row // head_count == block) & (row % head_count == lane // (width_all // head_count))
    lanes = jnp.where(here, 1.0, 0.0).astype(bf16)
    high, low = halves(jnp.exp(run_col_block))
    return dot(high, lanes) + dot(low, lanes)


def normed(values, gain):
    square = jnp.mean(values * values, axis=-1, keepdims=True)
    return values * lax.rsqrt(square + 1e-05) * gain


def swap_matrix(count, inner, turn=0):
    outer = count // inner
    place, source = iota((count, count), 0), iota((count, count), 1)
    return jnp.where(((place + turn) % outer) * inner + place // outer == source, 1.0, 0.0).astype(bf16)


def finish_rows(outputs, reach, proj, states, spans, came, gain, swap, lines):
    line_count, width_all = spans.shape
    state_count = states.shape[0] // line_count
    count = outputs.shape[0]
    width = count // line_count
    head_count = proj.shape[1] - 2 * state_count
    done = []
    for r in range(line_count):
        at = line_rows(r, state_count)
        state = states[at, :] + spans[r : r + 1, :] * came[at, :].astype(f32)
        padded = jnp.concatenate(
            [
                jnp.zeros((state_count, width_all), f32),
                state,
                jnp.zeros((head_count, width_all), f32),
            ],
            axis=0,
        )
        rows = slice(r * width, (r + 1) * width)
        whole = outputs[rows, :] + dot3(proj[rows, :], padded) * reach[rows, :]
        done.append(normed(whole, gain[...]).astype(bf16))
    lines[...] = dot(swap[...], jnp.concatenate(done, axis=0)).astype(bf16)


def put_turned(ref, start, rows):
    count, here = ref.shape[0], start % ref.shape[0]
    fits = min(count - here, rows.shape[0])
    ref[here : here + fits, :] = rows[:fits]
    if fits < rows.shape[0]:
        ref[: rows.shape[0] - fits, :] = rows[fits:]


def scan_columns(first, last, lines, w_proj, bias, rates, skips, outputs):
    count, width_all = lines.shape
    head_count = bias.shape[-1]
    inputs = lines[...]
    if first:
        inputs = jnp.concatenate([inputs[count - first :], inputs[: count - first]], axis=0)
    proj = dot_t(inputs, w_proj[...])
    proj_rows = dot_t(w_proj[...], inputs)
    state_count = (proj.shape[1] - head_count) // 2
    running, less, totals = step_terms(proj_rows, bias[...], rates[...], LANES)
    run_col = jnp.transpose(running)
    to_end = jnp.exp(totals - less)
    total_cols = jnp.transpose(totals)
    lanes = head_lanes(head_count, width_all // head_count)
    skip = spread(skips[...], lanes)
    blocks = count // LANES
    shape = (8, blocks * head_count)
    here = iota(shape, 1) // head_count == iota(shape, 0)
    picked = jnp.where(here, jnp.broadcast_to(total_cols[:1], shape), 0.0)
    decays = jnp.exp(by_ones(picked, jnp.concatenate([lanes] * blocks, axis=0).astype(bf16)))
    state = jnp.zeros((state_count, width_all), f32)
    for k in range(blocks):
        at = slice(k * LANES, (k + 1) * LANES)
        block = inputs[at]
        b_block = proj_rows[:state_count, at]
        own = within(proj[at], b_block, LANES, run_col, less, block, k, head_count)
        own = own + skip * block.astype(f32)
        if k > 0:
            padded = jnp.concatenate(
                [
                    jnp.zeros((state_count, width_all), f32),
                    state,
                    jnp.zeros((head_count, width_all), f32),
                ],
                axis=0,
            )
            own = own + dot3(proj[at], padded) * reach_lanes(
                run_col, k, head_count, width_all
            )
        put_turned(outputs, k * LANES - last, own.astype(bf16))
        if k + 1 < blocks:
            left = pushes(b_block, to_end, LANES, block, k, head_count)[0]
            state = decays[k : k + 1] * state + left


def make_gate(width, turn):
    def gate(masked, w_gate, gates, swap, back):
        value = dot(masked[...], w_gate[...])
        gates[...] = value / (1.0 + jnp.exp(-value))
        count = masked.shape[0]
        swap[...] = swap_matrix(count, width)
        back[...] = swap_matrix(count, count // width, turn)

    return gate


def finish(columns, gates, masked, w_out, gain, back, mixed, rows_out, sems):
    act = (normed(dot(back[...], columns[...]), gain[...]) * gates[...]).astype(bf16)
    copies = []
    part = mixed.shape[1] // sems.shape[0]
    for k in range(sems.shape[0]):
        at = slice(k * part, (k + 1) * part)
        rows_out[:, at] = (masked[:, at].astype(f32) + dot(act, w_out[:, at])).astype(bf16)
        copies.append(pltpu.make_async_copy(rows_out.at[:, at], mixed.at[:, at], sems.at[k]))
        copies[-1].start()
    for copy in copies:
        copy.wait()


def shifted(value, axis, by):
    count = lax.axis_size(axis)
    return lax.ppermute(value, axis, [(i, i + by) for i in range(count - by)])


IN_VMEM = pl.BlockSpec(memory_space=pltpu.VMEM)
IN_PLACE = pl.BlockSpec(memory_space=pltpu.HBM)


def call(body, out_shape, *args, flops=0, name=None, ins=IN_VMEM, outs=IN_VMEM, scratch=()):
    single = not isinstance(out_shape, tuple)
    return pl.pallas_call(
        body,
        out_shape=out_shape,
        in_specs=[ins] * len(args),
        out_specs=outs if single else tuple(outs for _ in out_shape),
        scratch_shapes=scratch,
        name=name,
        cost_estimate=pl.CostEstimate(flops=flops, bytes_accessed=4 << 20, transcendentals=0),
        compiler_params=pltpu.CompilerParams(vmem_limit_bytes=24 << 20),
    )(*args)


def on_device(
    patches,
    tissue,
    w_value,
    w_across,
    w_down,
    w_gate,
    w_out,
    step_bias_across,
    step_bias_down,
    rates_across,
    rates_down,
    skip_across,
    skip_down,
    gain_across,
    gain_final,
):
    shape = jax.ShapeDtypeStruct
    line_count, width, width_all = patches.shape
    count = line_count * width
    head_count = rates_across.shape[0]
    proj_count = w_across.shape[1]
    state_count = (proj_count - head_count) // 2
    blocks = count // LANES
    row = lambda x: x.reshape(1, -1)
    state_rows = line_count * state_count
    given = (
        patches.reshape(count, width_all),
        tissue,
        w_value,
        w_across.T,
        row(step_bias_across),
        row(rates_across),
    )
    masked, values, proj, b_rows, run_col, less_row, payload = call(
        prepare,
        (
            shape((count, width_all), bf16),
            shape((count, width_all), bf16),
            shape((count, proj_count), f32),
            shape((state_count, count), f32),
            shape((LANES, blocks * head_count), f32),
            shape((blocks * head_count, LANES), f32),
            shape((state_rows + 2 * line_count, width_all), bf16),
        ),
        *(pltpu.with_memory_space_constraint(x, pltpu.HBM) for x in given),
        flops=5 * 10**8,
        name="prepare",
        ins=IN_PLACE,
        scratch=[pltpu.VMEM(x.shape, x.dtype) for x in given]
        + [pltpu.SemaphoreType.DMA((len(given),))],
    )
    came = shifted(payload, "cols", 1)
    state, span, sent = call(
        first_step,
        (
            shape((state_rows, width_all), f32),
            shape((line_count, width_all), f32),
            shape(payload.shape, bf16),
        ),
        payload,
        came,
        flops=10**6,
        name="first_step",
    )
    came = shifted(sent, "cols", 2)
    early, _ = lax.optimization_barrier((masked, sent))
    gates, swap, back = call(
        make_gate(width, FIRST_DOWN - FIRST_BACK + width),
        (
            shape((count, width_all), f32),
            shape((count, count), bf16),
            shape((count, count), bf16),
        ),
        early,
        w_gate,
        flops=5 * 10**8,
        name="gate",
    )
    came, gates = lax.optimization_barrier((came, gates))
    states, spans, sent = call(
        second_step,
        (
            shape((state_rows, width_all), f32),
            shape((line_count, width_all), f32),
            shape((state_rows, width_all), bf16),
        ),
        payload,
        came,
        state,
        span,
        flops=10**6,
        name="second_step",
    )
    came = shifted(sent, "cols", 4)
    values, _ = lax.optimization_barrier((values, sent))
    passed = tuple(
        row(x) for x in (step_bias_down, rates_down, skip_down, gain_across, gain_final)
    )
    outputs, reach, bias_down, rate_down, skips_down, gains_across, gains_final = call(
        make_within(width),
        (shape((count, width_all), f32), shape((count, width_all), f32))
        + tuple(shape(x.shape, x.dtype) for x in passed),
        values,
        proj,
        b_rows,
        run_col,
        less_row,
        row(skip_across),
        *passed,
        flops=10**9,
        name="within_rows",
    )
    lines = call(
        finish_rows,
        shape((count, width_all), bf16),
        outputs,
        reach,
        proj,
        states,
        spans,
        came,
        gains_across,
        swap,
        flops=5 * 10**8,
        name="finish_rows",
    )
    split = (count // line_count, line_count, width_all)
    bands = lax.axis_size("rows")
    order = lambda first: [[(i + first) % bands for i in range(bands)]]
    exchange = lambda x, first: lax.all_to_all(
        x.reshape(split), "rows", 0, 0, axis_index_groups=order(first), tiled=True
    )
    lines = exchange(lines, FIRST_DOWN)
    columns = call(
        functools.partial(scan_columns, FIRST_DOWN * line_count, FIRST_BACK * line_count),
        shape((count, width_all), bf16),
        lines.reshape(count, width_all),
        w_down.T,
        bias_down,
        rate_down,
        skips_down,
        flops=10**9,
        name="scan_columns",
    )
    columns = exchange(columns, FIRST_BACK)
    mixed = call(
        finish,
        shape((count, width_all), bf16),
        columns.reshape(count, width_all),
        gates,
        masked,
        w_out,
        gains_final,
        back,
        flops=5 * 10**8,
        name="finish",
        outs=IN_PLACE,
        scratch=[
            pltpu.VMEM((count, width_all), bf16),
            pltpu.SemaphoreType.DMA((2,)),
        ],
    )
    return mixed.reshape(patches.shape)


def solution(mesh):
    return jax.shard_map(
        on_device,
        mesh=mesh,
        in_specs=(P("rows", "cols", None), P("rows", "cols")) + (P(),) * 13,
        out_specs=P("rows", "cols", None),
        check_vma=False,
    )
```

```python
import functools

import jax
import jax.numpy as jnp
from jax import lax
from jax.experimental import pallas as pl
from jax.experimental.pallas import tpu as pltpu
from jax.sharding import PartitionSpec as P

bf16, f32 = jnp.bfloat16, jnp.float32
LANES = 128
CAP = 80.0
FIRST_DOWN = 46
FIRST_BACK = 46


def iota(shape, dim):
    return lax.broadcasted_iota(jnp.int32, shape, dim)


def dot(a, b):
    return jnp.dot(a, b, preferred_element_type=f32)


def dot_t(a, b):
    return lax.dot_general(a, b, (((1,), (1,)), ((), ())), preferred_element_type=f32)


def halves(x):
    high = x.astype(bf16)
    return high, (x - high.astype(f32)).astype(bf16)


def softplus(v):
    return jnp.maximum(v, 0.0) + jnp.log1p(jnp.exp(-jnp.abs(v)))


def dot3(a, b):
    (ah, al), (bh, bl) = halves(a), halves(b)
    return dot(ah, bh) + (dot(al, bh) + dot(ah, bl))


def by_ones(a, ones):
    high, rest = a.astype(bf16), None
    rest = a - high.astype(f32)
    middle = rest.astype(bf16)
    low = (rest - middle.astype(f32)).astype(bf16)
    n = a.shape[0]
    whole = dot(jnp.concatenate([high.astype(f32), middle.astype(f32), low.astype(f32)], axis=0).astype(bf16), ones)
    return whole[:n] + (whole[n : 2 * n] + whole[2 * n :])


def as_column(row):
    n = row.shape[-1]
    square = jnp.broadcast_to(row, (n, n))
    return jnp.sum(jnp.where(iota((n, n), 0) == iota((n, n), 1), square, 0.0), axis=1, keepdims=True)


def head_lanes(head_count, width):
    shape = (head_count, head_count * width)
    return jnp.where(iota(shape, 1) // width == iota(shape, 0), 1.0, 0.0)


def step_terms(proj_rows, bias, rates, group):
    head_count = bias.shape[-1]
    steps = softplus(proj_rows[-head_count:] + as_column(bias))
    falls = -steps * as_column(rates)
    logs = jnp.log(steps)
    blocks = proj_rows.shape[1] // LANES
    stack = lambda x: jnp.concatenate([x[:, k * LANES : (k + 1) * LANES] for k in range(blocks)], axis=0)
    falls, logs = stack(falls), stack(logs)
    source, target = iota((LANES, LANES), 0), iota((LANES, LANES), 1)
    same = source // group == target // group
    running = by_ones(falls, jnp.where(same & (source <= target), 1.0, 0.0).astype(bf16))
    totals = by_ones(falls, jnp.where(same, 1.0, 0.0).astype(bf16))
    return running, running - logs, totals


def products(proj_block, b_block):
    state_count = b_block.shape[0]
    rest = proj_block.shape[1] - 2 * state_count
    padded = jnp.concatenate(
        [jnp.zeros_like(b_block), b_block, jnp.zeros((rest, b_block.shape[1]), f32)], axis=0
    )
    return dot3(proj_block, padded)


def within(proj_block, b_block, group, run_col, less_row, values, block, head_count):
    source, target = iota((LANES, LANES), 1), iota((LANES, LANES), 0)
    keep = (source // group == target // group) & (source <= target)
    inter = jnp.where(keep, products(proj_block, b_block), 0.0)
    low_lanes = iota((LANES, LANES), 1) < LANES // 2
    tiles = []
    for pair in range(head_count // 2):
        weights = []
        for head in (2 * pair, 2 * pair + 1):
            at = block * head_count + head
            spans = run_col[:, at : at + 1] - less_row[at : at + 1, :]
            weights.append((jnp.exp(jnp.minimum(spans, CAP)) * inter).astype(bf16))
        both = dot(jnp.concatenate(weights, axis=0), values[:, pair * LANES : (pair + 1) * LANES])
        tiles.append(jnp.where(low_lanes, both[:LANES], both[LANES:]))
    return jnp.concatenate(tiles, axis=1)


def pushes(b_block, to_end, group, values, block, head_count):
    state_count = b_block.shape[0]
    groups = LANES // group
    lane = iota((state_count, LANES), 1)
    tiles = [[] for _ in range(groups)]
    for pair in range(head_count // 2):
        rows = []
        for g in range(groups):
            for head in (2 * pair, 2 * pair + 1):
                at = block * head_count + head
                coef = b_block * to_end[at : at + 1, :]
                rows.append(jnp.where(lane // group == g, coef, 0.0).astype(bf16))
        left = dot(jnp.concatenate(rows, axis=0), values[:, pair * LANES : (pair + 1) * LANES])
        for g in range(groups):
            top = left[2 * g * state_count : (2 * g + 1) * state_count]
            bottom = left[(2 * g + 1) * state_count : (2 * g + 2) * state_count]
            tiles[g].append(jnp.where(lane < LANES // 2, top, bottom))
    return [jnp.concatenate(t, axis=1) for t in tiles]


def fetch(sources, targets, sems):
    copies = [
        pltpu.make_async_copy(source, target, sems.at[i])
        for i, (source, target) in enumerate(zip(sources, targets))
    ]
    for copy in copies:
        copy.start()
    return copies


def prepare(*refs):
    patches, tissue, w_value, w_proj, bias, rates = refs[:6]
    masked, values, b_rows, run_row, less_row, payload = refs[6:12]
    patches_in, tissue_in, value_in, proj_in, bias_in, rates_in, sems = refs[12:]
    copies = fetch(
        (tissue, patches, w_proj, bias, rates, w_value),
        (tissue_in, patches_in, proj_in, bias_in, rates_in, value_in),
        sems,
    )
    line_count, width = tissue_in.shape
    head_count = bias_in.shape[-1]
    copies[0].wait()
    flags = jnp.transpose(tissue_in[...].astype(f32))
    copies[1].wait()
    for r in range(line_count):
        keep = jnp.broadcast_to(flags[:, r : r + 1], (width, patches_in.shape[1])).astype(bf16)
        rows = slice(r * width, (r + 1) * width)
        masked[rows, :] = patches_in[rows, :] * keep
    inputs = masked[...]
    for copy in copies[2:5]:
        copy.wait()
    proj_rows = dot_t(proj_in[...], inputs)
    state_count = b_rows.shape[0]
    b_rows[...] = proj_rows[:state_count]
    running, less, totals = step_terms(proj_rows, bias_in[...], rates_in[...], width)
    less_row[...] = less
    run_row[...] = running
    to_end = jnp.exp(totals - less)
    total_cols = jnp.transpose(totals)
    blocks = inputs.shape[0] // LANES
    groups = LANES // width
    shape = (line_count, blocks * head_count)
    line, column = iota(shape, 0), iota(shape, 1)
    picked = jnp.zeros(shape, f32)
    for g in range(groups):
        here = (line % groups == g) & (column // head_count == line // groups)
        picked = jnp.where(here, total_cols[g * width : g * width + 1, :], picked)
    lanes = jnp.concatenate([head_lanes(head_count, inputs.shape[1] // head_count)] * blocks, axis=0)
    decays = jnp.exp(by_ones(picked, lanes.astype(bf16)))
    keep_decays(payload, decays)
    copies[5].wait()
    narrow = dot(inputs, value_in[...]).astype(bf16)
    values[...] = narrow
    for k in range(blocks):
        at = slice(k * LANES, (k + 1) * LANES)
        left = pushes(proj_rows[:state_count, at], to_end, width, narrow[at], k, head_count)
        for g in range(groups):
            r = k * groups + g
            payload[r * state_count : (r + 1) * state_count, :] = left[g].astype(bf16)


def keep_decays(payload, decays):
    high, low = halves(decays)
    pair = jnp.concatenate([high.astype(f32), low.astype(f32)], axis=0).astype(bf16)
    payload[payload.shape[0] - pair.shape[0] :, :] = pair


def read_decays(payload, line_count):
    pair = payload[payload.shape[0] - 2 * line_count :, :].astype(f32)
    return pair[:line_count] + pair[line_count:]


def line_rows(r, state_count):
    return slice(r * state_count, (r + 1) * state_count)


def first_step(own, came, state, span, sent):
    line_count = span.shape[0]
    state_count = state.shape[0] // line_count
    decays, before = read_decays(own, line_count), read_decays(came, line_count)
    span[...] = before
    keep_decays(sent, decays * before)
    for r in range(line_count):
        at = line_rows(r, state_count)
        entered = came[at, :].astype(f32)
        state[at, :] = entered
        sent[at, :] = (own[at, :].astype(f32) + decays[r : r + 1] * entered).astype(bf16)


def second_step(own, came, state, span, states, spans, sent):
    line_count = span.shape[0]
    state_count = state.shape[0] // line_count
    decays, before = read_decays(own, line_count), read_decays(came, line_count)
    over = span[...]
    spans[...] = over * before
    for r in range(line_count):
        at = line_rows(r, state_count)
        entered = state[at, :] + over[r : r + 1] * came[at, :].astype(f32)
        states[at, :] = entered
        sent[at, :] = (own[at, :].astype(f32) + decays[r : r + 1] * entered).astype(bf16)


def spread(row, lanes):
    return by_ones(jnp.broadcast_to(row, (8, row.shape[-1])), lanes.astype(bf16))[:1]


def make_within(group):
    def body(values, proj, b_rows, run_row, less_row, skips, *refs):
        given, (outputs, reach), passed = refs[:4], refs[4:6], refs[6:]
        run_col = jnp.transpose(run_row[...])
        for source, target in zip(given, passed):
            target[...] = source[...]
        head_count = skips.shape[-1]
        count, width_all = values.shape
        skip = spread(skips[...], head_lanes(head_count, width_all // head_count))
        for k in range(count // LANES):
            at = slice(k * LANES, (k + 1) * LANES)
            block = values[at, :]
            own = within(
                proj[at, :], b_rows[:, at], group, run_col, less_row[...], block, k, head_count
            )
            outputs[at, :] = own + skip * block.astype(f32)
            reach[at, :] = reach_lanes(run_col, k, head_count, width_all)

    return body


def reach_lanes(run_col_block, block, head_count, width_all):
    shape = (run_col_block.shape[1], width_all)
    row, lane = iota(shape, 0), iota(shape, 1)
    here = (row // head_count == block) & (row % head_count == lane // (width_all // head_count))
    lanes = jnp.where(here, 1.0, 0.0).astype(bf16)
    high, low = halves(jnp.exp(run_col_block))
    return dot(high, lanes) + dot(low, lanes)


def normed(values, gain):
    square = jnp.mean(values * values, axis=-1, keepdims=True)
    return values * lax.rsqrt(square + 1e-05) * gain


def swap_matrix(count, inner, turn=0):
    outer = count // inner
    place, source = iota((count, count), 0), iota((count, count), 1)
    return jnp.where(((place + turn) % outer) * inner + place // outer == source, 1.0, 0.0).astype(bf16)


def finish_rows(outputs, reach, proj, states, spans, came, gain, swap, lines):
    line_count, width_all = spans.shape
    state_count = states.shape[0] // line_count
    count = outputs.shape[0]
    width = count // line_count
    head_count = proj.shape[1] - 2 * state_count
    done = []
    for r in range(line_count):
        at = line_rows(r, state_count)
        state = states[at, :] + spans[r : r + 1, :] * came[at, :].astype(f32)
        padded = jnp.concatenate(
            [
                jnp.zeros((state_count, width_all), f32),
                state,
                jnp.zeros((head_count, width_all), f32),
            ],
            axis=0,
        )
        rows = slice(r * width, (r + 1) * width)
        whole = outputs[rows, :] + dot3(proj[rows, :], padded) * reach[rows, :]
        done.append(normed(whole, gain[...]).astype(bf16))
    lines[...] = dot(swap[...], jnp.concatenate(done, axis=0)).astype(bf16)


def put_turned(ref, start, rows):
    count, here = ref.shape[0], start % ref.shape[0]
    fits = min(count - here, rows.shape[0])
    ref[here : here + fits, :] = rows[:fits]
    if fits < rows.shape[0]:
        ref[: rows.shape[0] - fits, :] = rows[fits:]


def scan_columns(first, last, lines, w_proj, bias, rates, skips, outputs):
    count, width_all = lines.shape
    head_count = bias.shape[-1]
    inputs = lines[...]
    if first:
        inputs = jnp.concatenate([inputs[count - first :], inputs[: count - first]], axis=0)
    proj = dot_t(inputs, w_proj[...])
    proj_rows = dot_t(w_proj[...], inputs)
    state_count = (proj.shape[1] - head_count) // 2
    running, less, totals = step_terms(proj_rows, bias[...], rates[...], LANES)
    run_col = jnp.transpose(running)
    to_end = jnp.exp(totals - less)
    total_cols = jnp.transpose(totals)
    lanes = head_lanes(head_count, width_all // head_count)
    skip = spread(skips[...], lanes)
    blocks = count // LANES
    shape = (8, blocks * head_count)
    here = iota(shape, 1) // head_count == iota(shape, 0)
    picked = jnp.where(here, jnp.broadcast_to(total_cols[:1], shape), 0.0)
    decays = jnp.exp(by_ones(picked, jnp.concatenate([lanes] * blocks, axis=0).astype(bf16)))
    state = jnp.zeros((state_count, width_all), f32)
    for k in range(blocks):
        at = slice(k * LANES, (k + 1) * LANES)
        block = inputs[at]
        b_block = proj_rows[:state_count, at]
        own = within(proj[at], b_block, LANES, run_col, less, block, k, head_count)
        own = own + skip * block.astype(f32)
        if k > 0:
            padded = jnp.concatenate(
                [
                    jnp.zeros((state_count, width_all), f32),
                    state,
                    jnp.zeros((head_count, width_all), f32),
                ],
                axis=0,
            )
            own = own + dot3(proj[at], padded) * reach_lanes(
                run_col, k, head_count, width_all
            )
        put_turned(outputs, k * LANES - last, own.astype(bf16))
        if k + 1 < blocks:
            left = pushes(b_block, to_end, LANES, block, k, head_count)[0]
            state = decays[k : k + 1] * state + left


def make_gate(width, turn):
    def gate(masked, w_gate, w_proj, gain, gates, proj, swap, back):
        proj[...] = dot_t(masked[...], w_proj[...])
        value = dot(masked[...], w_gate[...])
        gates[...] = gain[...] * (value / (1.0 + jnp.exp(-value)))
        count = masked.shape[0]
        swap[...] = swap_matrix(count, width)
        back[...] = swap_matrix(count, count // width, turn)

    return gate


def finish(columns, gates, masked, w_out, back, mixed, rows_out, sems):
    act = normed(dot(back[...], columns[...]), gates[...]).astype(bf16)
    copies = []
    part = mixed.shape[1] // sems.shape[0]
    for k in range(sems.shape[0]):
        at = slice(k * part, (k + 1) * part)
        rows_out[:, at] = (masked[:, at].astype(f32) + dot(act, w_out[:, at])).astype(bf16)
        copies.append(pltpu.make_async_copy(rows_out.at[:, at], mixed.at[:, at], sems.at[k]))
        copies[-1].start()
    for copy in copies:
        copy.wait()


def shifted(value, axis, by):
    count = lax.axis_size(axis)
    return lax.ppermute(value, axis, [(i, i + by) for i in range(count - by)])


IN_VMEM = pl.BlockSpec(memory_space=pltpu.VMEM)
IN_PLACE = pl.BlockSpec(memory_space=pltpu.HBM)


def call(body, out_shape, *args, flops=0, name=None, ins=IN_VMEM, outs=IN_VMEM, scratch=()):
    single = not isinstance(out_shape, tuple)
    return pl.pallas_call(
        body,
        out_shape=out_shape,
        in_specs=[ins] * len(args),
        out_specs=outs if single else tuple(outs for _ in out_shape),
        scratch_shapes=scratch,
        name=name,
        cost_estimate=pl.CostEstimate(flops=flops, bytes_accessed=4 << 20, transcendentals=0),
        compiler_params=pltpu.CompilerParams(vmem_limit_bytes=24 << 20),
    )(*args)


def on_device(
    patches,
    tissue,
    w_value,
    w_across,
    w_down,
    w_gate,
    w_out,
    step_bias_across,
    step_bias_down,
    rates_across,
    rates_down,
    skip_across,
    skip_down,
    gain_across,
    gain_final,
):
    shape = jax.ShapeDtypeStruct
    line_count, width, width_all = patches.shape
    count = line_count * width
    head_count = rates_across.shape[0]
    proj_count = w_across.shape[1]
    state_count = (proj_count - head_count) // 2
    blocks = count // LANES
    row = lambda x: x.reshape(1, -1)
    state_rows = line_count * state_count
    given = (
        patches.reshape(count, width_all),
        tissue,
        w_value,
        w_across.T,
        row(step_bias_across),
        row(rates_across),
    )
    masked, values, b_rows, run_row, less_row, payload = call(
        prepare,
        (
            shape((count, width_all), bf16),
            shape((count, width_all), bf16),
            shape((state_count, count), f32),
            shape((blocks * head_count, LANES), f32),
            shape((blocks * head_count, LANES), f32),
            shape((state_rows + 2 * line_count, width_all), bf16),
        ),
        *(pltpu.with_memory_space_constraint(x, pltpu.HBM) for x in given),
        flops=5 * 10**8,
        name="prepare",
        ins=IN_PLACE,
        scratch=[pltpu.VMEM(x.shape, x.dtype) for x in given]
        + [pltpu.SemaphoreType.DMA((len(given),))],
    )
    came = shifted(payload, "cols", 1)
    state, span, sent = call(
        first_step,
        (
            shape((state_rows, width_all), f32),
            shape((line_count, width_all), f32),
            shape(payload.shape, bf16),
        ),
        payload,
        came,
        flops=10**6,
        name="first_step",
    )
    came = shifted(sent, "cols", 2)
    early, _ = lax.optimization_barrier((masked, sent))
    gates, proj, swap, back = call(
        make_gate(width, FIRST_DOWN - FIRST_BACK + width),
        (
            shape((count, width_all), f32),
            shape((count, proj_count), f32),
            shape((count, count), bf16),
            shape((count, count), bf16),
        ),
        early,
        w_gate,
        w_across.T,
        row(gain_final),
        flops=5 * 10**8,
        name="gate",
    )
    came, gates = lax.optimization_barrier((came, gates))
    states, spans, sent = call(
        second_step,
        (
            shape((state_rows, width_all), f32),
            shape((line_count, width_all), f32),
            shape((state_rows, width_all), bf16),
        ),
        payload,
        came,
        state,
        span,
        flops=10**6,
        name="second_step",
    )
    came = shifted(sent, "cols", 4)
    values, _ = lax.optimization_barrier((values, sent))
    passed = tuple(
        row(x) for x in (step_bias_down, rates_down, skip_down, gain_across)
    )
    outputs, reach, bias_down, rate_down, skips_down, gains_across = call(
        make_within(width),
        (shape((count, width_all), f32), shape((count, width_all), f32))
        + tuple(shape(x.shape, x.dtype) for x in passed),
        values,
        proj,
        b_rows,
        run_row,
        less_row,
        row(skip_across),
        *passed,
        flops=10**9,
        name="within_rows",
    )
    lines = call(
        finish_rows,
        shape((count, width_all), bf16),
        outputs,
        reach,
        proj,
        states,
        spans,
        came,
        gains_across,
        swap,
        flops=5 * 10**8,
        name="finish_rows",
    )
    split = (count // line_count, line_count, width_all)
    bands = lax.axis_size("rows")
    order = lambda first: [[(i + first) % bands for i in range(bands)]]
    exchange = lambda x, first: lax.all_to_all(
        x.reshape(split), "rows", 0, 0, axis_index_groups=order(first), tiled=True
    )
    lines = exchange(lines, FIRST_DOWN)
    columns = call(
        functools.partial(scan_columns, FIRST_DOWN * line_count, FIRST_BACK * line_count),
        shape((count, width_all), bf16),
        lines.reshape(count, width_all),
        w_down.T,
        bias_down,
        rate_down,
        skips_down,
        flops=10**9,
        name="scan_columns",
    )
    columns = exchange(columns, FIRST_BACK)
    mixed = call(
        finish,
        shape((count, width_all), bf16),
        columns.reshape(count, width_all),
        gates,
        masked,
        w_out,
        back,
        flops=5 * 10**8,
        name="finish",
        outs=IN_PLACE,
        scratch=[
            pltpu.VMEM((count, width_all), bf16),
            pltpu.SemaphoreType.DMA((2,)),
        ],
    )
    return mixed.reshape(patches.shape)


def solution(mesh):
    return jax.shard_map(
        on_device,
        mesh=mesh,
        in_specs=(P("rows", "cols", None), P("rows", "cols")) + (P(),) * 13,
        out_specs=P("rows", "cols", None),
        check_vma=False,
    )
```

```python
import functools

import jax
import jax.numpy as jnp
from jax import lax
from jax.experimental import pallas as pl
from jax.experimental.pallas import tpu as pltpu
from jax.sharding import PartitionSpec as P

bf16, f32 = jnp.bfloat16, jnp.float32
LANES = 128
CAP = 80.0
FIRST_DOWN = 46
FIRST_BACK = 46


def iota(shape, dim):
    return lax.broadcasted_iota(jnp.int32, shape, dim)


def dot(a, b):
    return jnp.dot(a, b, preferred_element_type=f32)


def dot_t(a, b):
    return lax.dot_general(a, b, (((1,), (1,)), ((), ())), preferred_element_type=f32)


def halves(x):
    high = x.astype(bf16)
    return high, (x - high.astype(f32)).astype(bf16)


def softplus(v):
    return jnp.maximum(v, 0.0) + jnp.log1p(jnp.exp(-jnp.abs(v)))


def dot3(a, b):
    (ah, al), (bh, bl) = halves(a), halves(b)
    return dot(ah, bh) + (dot(al, bh) + dot(ah, bl))


def by_ones(a, ones):
    high, rest = a.astype(bf16), None
    rest = a - high.astype(f32)
    middle = rest.astype(bf16)
    low = (rest - middle.astype(f32)).astype(bf16)
    n = a.shape[0]
    whole = dot(jnp.concatenate([high.astype(f32), middle.astype(f32), low.astype(f32)], axis=0).astype(bf16), ones)
    return whole[:n] + (whole[n : 2 * n] + whole[2 * n :])


def as_column(row):
    n = row.shape[-1]
    square = jnp.broadcast_to(row, (n, n))
    return jnp.sum(jnp.where(iota((n, n), 0) == iota((n, n), 1), square, 0.0), axis=1, keepdims=True)


def head_lanes(head_count, width):
    shape = (head_count, head_count * width)
    return jnp.where(iota(shape, 1) // width == iota(shape, 0), 1.0, 0.0)


def step_terms(proj_rows, bias, rates, group):
    head_count = bias.shape[-1]
    steps = softplus(proj_rows[-head_count:] + as_column(bias))
    falls = -steps * as_column(rates)
    logs = jnp.log(steps)
    blocks = proj_rows.shape[1] // LANES
    stack = lambda x: jnp.concatenate([x[:, k * LANES : (k + 1) * LANES] for k in range(blocks)], axis=0)
    falls, logs = stack(falls), stack(logs)
    source, target = iota((LANES, LANES), 0), iota((LANES, LANES), 1)
    same = source // group == target // group
    running = by_ones(falls, jnp.where(same & (source <= target), 1.0, 0.0).astype(bf16))
    totals = by_ones(falls, jnp.where(same, 1.0, 0.0).astype(bf16))
    return running, running - logs, totals


def products(proj_block, b_block):
    state_count = b_block.shape[0]
    rest = proj_block.shape[1] - 2 * state_count
    padded = jnp.concatenate(
        [jnp.zeros_like(b_block), b_block, jnp.zeros((rest, b_block.shape[1]), f32)], axis=0
    )
    return dot3(proj_block, padded)


def within(proj_block, b_block, group, run_col, less_row, values, block, head_count):
    source, target = iota((LANES, LANES), 1), iota((LANES, LANES), 0)
    keep = (source // group == target // group) & (source <= target)
    inter = jnp.where(keep, products(proj_block, b_block), 0.0)
    low_lanes = iota((LANES, LANES), 1) < LANES // 2
    tiles = []
    for pair in range(head_count // 2):
        weights = []
        for head in (2 * pair, 2 * pair + 1):
            at = block * head_count + head
            spans = run_col[:, at : at + 1] - less_row[at : at + 1, :]
            weights.append((jnp.exp(jnp.minimum(spans, CAP)) * inter).astype(bf16))
        both = dot(jnp.concatenate(weights, axis=0), values[:, pair * LANES : (pair + 1) * LANES])
        tiles.append(jnp.where(low_lanes, both[:LANES], both[LANES:]))
    return jnp.concatenate(tiles, axis=1)


def pushes(b_block, to_end, group, values, block, head_count):
    state_count = b_block.shape[0]
    groups = LANES // group
    lane = iota((state_count, LANES), 1)
    tiles = [[] for _ in range(groups)]
    for pair in range(head_count // 2):
        rows = []
        for g in range(groups):
            for head in (2 * pair, 2 * pair + 1):
                at = block * head_count + head
                coef = b_block * to_end[at : at + 1, :]
                rows.append(jnp.where(lane // group == g, coef, 0.0).astype(bf16))
        left = dot(jnp.concatenate(rows, axis=0), values[:, pair * LANES : (pair + 1) * LANES])
        for g in range(groups):
            top = left[2 * g * state_count : (2 * g + 1) * state_count]
            bottom = left[(2 * g + 1) * state_count : (2 * g + 2) * state_count]
            tiles[g].append(jnp.where(lane < LANES // 2, top, bottom))
    return [jnp.concatenate(t, axis=1) for t in tiles]


def fetch(sources, targets, sems):
    copies = [
        pltpu.make_async_copy(source, target, sems.at[i])
        for i, (source, target) in enumerate(zip(sources, targets))
    ]
    for copy in copies:
        copy.start()
    return copies


def prepare(*refs):
    patches, tissue, w_value, w_proj, bias, rates = refs[:6]
    masked, values, b_rows, run_row, less_row, payload = refs[6:12]
    patches_in, tissue_in, value_in, proj_in, bias_in, rates_in, sems = refs[12:]
    copies = fetch(
        (tissue, patches, w_proj, bias, rates, w_value),
        (tissue_in, patches_in, proj_in, bias_in, rates_in, value_in),
        sems,
    )
    line_count, width = tissue_in.shape
    head_count = bias_in.shape[-1]
    copies[0].wait()
    flags = jnp.transpose(tissue_in[...].astype(f32))
    copies[1].wait()
    for r in range(line_count):
        keep = jnp.broadcast_to(flags[:, r : r + 1], (width, patches_in.shape[1])).astype(bf16)
        rows = slice(r * width, (r + 1) * width)
        masked[rows, :] = patches_in[rows, :] * keep
    inputs = masked[...]
    for copy in copies[2:5]:
        copy.wait()
    proj_rows = dot_t(proj_in[...], inputs)
    state_count = b_rows.shape[0]
    b_rows[...] = proj_rows[:state_count]
    running, less, totals = step_terms(proj_rows, bias_in[...], rates_in[...], width)
    less_row[...] = less
    run_row[...] = running
    to_end = jnp.exp(totals - less)
    total_cols = jnp.transpose(totals)
    blocks = inputs.shape[0] // LANES
    groups = LANES // width
    shape = (line_count, blocks * head_count)
    line, column = iota(shape, 0), iota(shape, 1)
    picked = jnp.zeros(shape, f32)
    for g in range(groups):
        here = (line % groups == g) & (column // head_count == line // groups)
        picked = jnp.where(here, total_cols[g * width : g * width + 1, :], picked)
    lanes = jnp.concatenate([head_lanes(head_count, inputs.shape[1] // head_count)] * blocks, axis=0)
    decays = jnp.exp(by_ones(picked, lanes.astype(bf16)))
    keep_decays(payload, decays)
    copies[5].wait()
    narrow = dot(inputs, value_in[...]).astype(bf16)
    values[...] = narrow
    for k in range(blocks):
        at = slice(k * LANES, (k + 1) * LANES)
        left = pushes(proj_rows[:state_count, at], to_end, width, narrow[at], k, head_count)
        for g in range(groups):
            r = k * groups + g
            payload[r * state_count : (r + 1) * state_count, :] = left[g].astype(bf16)


def keep_decays(payload, decays):
    high, low = halves(decays)
    pair = jnp.concatenate([high.astype(f32), low.astype(f32)], axis=0).astype(bf16)
    payload[payload.shape[0] - pair.shape[0] :, :] = pair


def read_decays(payload, line_count):
    pair = payload[payload.shape[0] - 2 * line_count :, :].astype(f32)
    return pair[:line_count] + pair[line_count:]


def line_rows(r, state_count):
    return slice(r * state_count, (r + 1) * state_count)


def first_step(own, came, state, span, sent):
    line_count = span.shape[0]
    state_count = state.shape[0] // line_count
    later = lax.rem(lax.axis_index("cols"), 2) == 1
    mine, other = read_decays(own, line_count), read_decays(came, line_count)
    span[...] = jnp.where(later, other, 1.0)
    keep_decays(sent, mine * other)
    second = jnp.where(later, mine, other)
    for r in range(line_count):
        at = line_rows(r, state_count)
        here, there = own[at, :].astype(f32), came[at, :].astype(f32)
        state[at, :] = jnp.where(later, there, 0.0)
        head, tail = jnp.where(later, there, here), jnp.where(later, here, there)
        sent[at, :] = (tail + second[r : r + 1] * head).astype(bf16)


def second_step(own, came, state, span, states, spans, sent):
    line_count = span.shape[0]
    state_count = state.shape[0] // line_count
    decays, before = read_decays(own, line_count), read_decays(came, line_count)
    over = span[...]
    spans[...] = over * before
    for r in range(line_count):
        at = line_rows(r, state_count)
        entered = came[at, :].astype(f32)
        states[at, :] = state[at, :] + over[r : r + 1] * entered
        sent[at, :] = (own[at, :].astype(f32) + decays[r : r + 1] * entered).astype(bf16)


def spread(row, lanes):
    return by_ones(jnp.broadcast_to(row, (8, row.shape[-1])), lanes.astype(bf16))[:1]


def make_within(group):
    def body(values, proj, b_rows, run_row, less_row, skips, *refs):
        given, (outputs, reach), passed = refs[:4], refs[4:6], refs[6:]
        run_col = jnp.transpose(run_row[...])
        for source, target in zip(given, passed):
            target[...] = source[...]
        head_count = skips.shape[-1]
        count, width_all = values.shape
        skip = spread(skips[...], head_lanes(head_count, width_all // head_count))
        for k in range(count // LANES):
            at = slice(k * LANES, (k + 1) * LANES)
            block = values[at, :]
            own = within(
                proj[at, :], b_rows[:, at], group, run_col, less_row[...], block, k, head_count
            )
            outputs[at, :] = own + skip * block.astype(f32)
            reach[at, :] = reach_lanes(run_col, k, head_count, width_all)

    return body


def reach_lanes(run_col_block, block, head_count, width_all):
    shape = (run_col_block.shape[1], width_all)
    row, lane = iota(shape, 0), iota(shape, 1)
    here = (row // head_count == block) & (row % head_count == lane // (width_all // head_count))
    lanes = jnp.where(here, 1.0, 0.0).astype(bf16)
    high, low = halves(jnp.exp(run_col_block))
    return dot(high, lanes) + dot(low, lanes)


def normed(values, gain):
    square = jnp.mean(values * values, axis=-1, keepdims=True)
    return values * lax.rsqrt(square + 1e-05) * gain


def swap_matrix(count, inner, turn=0):
    outer = count // inner
    place, source = iota((count, count), 0), iota((count, count), 1)
    return jnp.where(((place + turn) % outer) * inner + place // outer == source, 1.0, 0.0).astype(bf16)


def finish_rows(outputs, reach, proj, states, spans, came, gain, swap, lines):
    line_count, width_all = spans.shape
    state_count = states.shape[0] // line_count
    count = outputs.shape[0]
    width = count // line_count
    head_count = proj.shape[1] - 2 * state_count
    done = []
    for r in range(line_count):
        at = line_rows(r, state_count)
        state = states[at, :] + spans[r : r + 1, :] * came[at, :].astype(f32)
        padded = jnp.concatenate(
            [
                jnp.zeros((state_count, width_all), f32),
                state,
                jnp.zeros((head_count, width_all), f32),
            ],
            axis=0,
        )
        rows = slice(r * width, (r + 1) * width)
        whole = outputs[rows, :] + dot3(proj[rows, :], padded) * reach[rows, :]
        done.append(normed(whole, gain[...]).astype(bf16))
    lines[...] = dot(swap[...], jnp.concatenate(done, axis=0)).astype(bf16)


def put_turned(ref, start, rows):
    count, here = ref.shape[0], start % ref.shape[0]
    fits = min(count - here, rows.shape[0])
    ref[here : here + fits, :] = rows[:fits]
    if fits < rows.shape[0]:
        ref[: rows.shape[0] - fits, :] = rows[fits:]


def scan_columns(first, last, lines, w_proj, bias, rates, skips, outputs):
    count, width_all = lines.shape
    head_count = bias.shape[-1]
    inputs = lines[...]
    if first:
        inputs = jnp.concatenate([inputs[count - first :], inputs[: count - first]], axis=0)
    proj = dot_t(inputs, w_proj[...])
    proj_rows = dot_t(w_proj[...], inputs)
    state_count = (proj.shape[1] - head_count) // 2
    running, less, totals = step_terms(proj_rows, bias[...], rates[...], LANES)
    run_col = jnp.transpose(running)
    to_end = jnp.exp(totals - less)
    total_cols = jnp.transpose(totals)
    lanes = head_lanes(head_count, width_all // head_count)
    skip = spread(skips[...], lanes)
    blocks = count // LANES
    shape = (8, blocks * head_count)
    here = iota(shape, 1) // head_count == iota(shape, 0)
    picked = jnp.where(here, jnp.broadcast_to(total_cols[:1], shape), 0.0)
    decays = jnp.exp(by_ones(picked, jnp.concatenate([lanes] * blocks, axis=0).astype(bf16)))
    state = jnp.zeros((state_count, width_all), f32)
    for k in range(blocks):
        at = slice(k * LANES, (k + 1) * LANES)
        block = inputs[at]
        b_block = proj_rows[:state_count, at]
        own = within(proj[at], b_block, LANES, run_col, less, block, k, head_count)
        own = own + skip * block.astype(f32)
        if k > 0:
            padded = jnp.concatenate(
                [
                    jnp.zeros((state_count, width_all), f32),
                    state,
                    jnp.zeros((head_count, width_all), f32),
                ],
                axis=0,
            )
            own = own + dot3(proj[at], padded) * reach_lanes(
                run_col, k, head_count, width_all
            )
        put_turned(outputs, k * LANES - last, own.astype(bf16))
        if k + 1 < blocks:
            left = pushes(b_block, to_end, LANES, block, k, head_count)[0]
            state = decays[k : k + 1] * state + left


def make_gate(width, turn):
    def gate(masked, w_gate, w_proj, gain, gates, proj, swap, back):
        proj[...] = dot_t(masked[...], w_proj[...])
        value = dot(masked[...], w_gate[...])
        gates[...] = gain[...] * (value / (1.0 + jnp.exp(-value)))
        count = masked.shape[0]
        swap[...] = swap_matrix(count, width)
        back[...] = swap_matrix(count, count // width, turn)

    return gate


def finish(columns, gates, masked, w_out, back, mixed, rows_out, sems):
    act = normed(dot(back[...], columns[...]), gates[...]).astype(bf16)
    copies = []
    part = mixed.shape[1] // sems.shape[0]
    for k in range(sems.shape[0]):
        at = slice(k * part, (k + 1) * part)
        rows_out[:, at] = (masked[:, at].astype(f32) + dot(act, w_out[:, at])).astype(bf16)
        copies.append(pltpu.make_async_copy(rows_out.at[:, at], mixed.at[:, at], sems.at[k]))
        copies[-1].start()
    for copy in copies:
        copy.wait()


def shifted(value, axis, by):
    count = lax.axis_size(axis)
    return lax.ppermute(value, axis, [(i, i + by) for i in range(count - by)])


IN_VMEM = pl.BlockSpec(memory_space=pltpu.VMEM)
IN_PLACE = pl.BlockSpec(memory_space=pltpu.HBM)


def on_core(core, body, skipped=0):
    def guarded(*refs):
        @pl.when(lax.rem(lax.axis_index("cols"), 2) == core)
        def _():
            body(*refs[skipped:])

    return guarded


def call(
    body, out_shape, *args, flops=0, name=None, ins=IN_VMEM, outs=IN_VMEM, scratch=(), aliases={}
):
    single = not isinstance(out_shape, tuple)
    return pl.pallas_call(
        body,
        out_shape=out_shape,
        in_specs=[ins] * len(args),
        out_specs=outs if single else tuple(outs for _ in out_shape),
        scratch_shapes=scratch,
        name=name,
        input_output_aliases=aliases,
        cost_estimate=pl.CostEstimate(flops=flops, bytes_accessed=4 << 20, transcendentals=0),
        compiler_params=pltpu.CompilerParams(vmem_limit_bytes=24 << 20),
    )(*args)


def on_device(
    patches,
    tissue,
    w_value,
    w_across,
    w_down,
    w_gate,
    w_out,
    step_bias_across,
    step_bias_down,
    rates_across,
    rates_down,
    skip_across,
    skip_down,
    gain_across,
    gain_final,
):
    shape = jax.ShapeDtypeStruct
    line_count, width, width_all = patches.shape
    count = line_count * width
    head_count = rates_across.shape[0]
    proj_count = w_across.shape[1]
    state_count = (proj_count - head_count) // 2
    blocks = count // LANES
    row = lambda x: x.reshape(1, -1)
    state_rows = line_count * state_count
    given = (
        patches.reshape(count, width_all),
        tissue,
        w_value,
        w_across.T,
        row(step_bias_across),
        row(rates_across),
    )
    masked, values, b_rows, run_row, less_row, payload = call(
        prepare,
        (
            shape((count, width_all), bf16),
            shape((count, width_all), bf16),
            shape((state_count, count), f32),
            shape((blocks * head_count, LANES), f32),
            shape((blocks * head_count, LANES), f32),
            shape((state_rows + 2 * line_count, width_all), bf16),
        ),
        *(pltpu.with_memory_space_constraint(x, pltpu.HBM) for x in given),
        flops=5 * 10**8,
        name="prepare",
        ins=IN_PLACE,
        scratch=[pltpu.VMEM(x.shape, x.dtype) for x in given]
        + [pltpu.SemaphoreType.DMA((len(given),))],
    )
    count_of = lax.axis_size("cols")
    came = lax.ppermute(payload, "cols", [(i, i ^ 1) for i in range(count_of)])
    state, span, sent = call(
        first_step,
        (
            shape((state_rows, width_all), f32),
            shape((line_count, width_all), f32),
            shape(payload.shape, bf16),
        ),
        payload,
        came,
        flops=10**6,
        name="first_step",
    )
    gate_shapes = (
        shape((count, width_all), f32),
        shape((count, proj_count), f32),
        shape((count, count), bf16),
        shape((count, count), bf16),
    )
    gate = make_gate(width, FIRST_DOWN - FIRST_BACK + width)
    early, _ = lax.optimization_barrier((masked, sent))
    gate_args = (early, w_gate, w_across.T, row(gain_final))
    half_made = call(
        on_core(0, gate), gate_shapes, *gate_args, flops=5 * 10**8, name="gate_first"
    )
    sent, half_made = lax.optimization_barrier((sent, half_made))
    came = shifted(sent, "cols", 2)
    gates, proj, swap, back = call(
        on_core(1, gate, 4),
        gate_shapes,
        *half_made,
        *gate_args,
        flops=5 * 10**8,
        name="gate_second",
        aliases={i: i for i in range(4)},
    )
    came, gates = lax.optimization_barrier((came, gates))
    states, spans, sent = call(
        second_step,
        (
            shape((state_rows, width_all), f32),
            shape((line_count, width_all), f32),
            shape((state_rows, width_all), bf16),
        ),
        sent,
        came,
        state,
        span,
        flops=10**6,
        name="second_step",
    )
    came = shifted(sent, "cols", 4)
    values, _ = lax.optimization_barrier((values, sent))
    passed = tuple(
        row(x) for x in (step_bias_down, rates_down, skip_down, gain_across)
    )
    outputs, reach, bias_down, rate_down, skips_down, gains_across = call(
        make_within(width),
        (shape((count, width_all), f32), shape((count, width_all), f32))
        + tuple(shape(x.shape, x.dtype) for x in passed),
        values,
        proj,
        b_rows,
        run_row,
        less_row,
        row(skip_across),
        *passed,
        flops=10**9,
        name="within_rows",
    )
    lines = call(
        finish_rows,
        shape((count, width_all), bf16),
        outputs,
        reach,
        proj,
        states,
        spans,
        came,
        gains_across,
        swap,
        flops=5 * 10**8,
        name="finish_rows",
    )
    split = (count // line_count, line_count, width_all)
    bands = lax.axis_size("rows")
    order = lambda first: [[(i + first) % bands for i in range(bands)]]
    exchange = lambda x, first: lax.all_to_all(
        x.reshape(split), "rows", 0, 0, axis_index_groups=order(first), tiled=True
    )
    lines = exchange(lines, FIRST_DOWN)
    columns = call(
        functools.partial(scan_columns, FIRST_DOWN * line_count, FIRST_BACK * line_count),
        shape((count, width_all), bf16),
        lines.reshape(count, width_all),
        w_down.T,
        bias_down,
        rate_down,
        skips_down,
        flops=10**9,
        name="scan_columns",
    )
    columns = exchange(columns, FIRST_BACK)
    mixed = call(
        finish,
        shape((count, width_all), bf16),
        columns.reshape(count, width_all),
        gates,
        masked,
        w_out,
        back,
        flops=5 * 10**8,
        name="finish",
        outs=IN_PLACE,
        scratch=[
            pltpu.VMEM((count, width_all), bf16),
            pltpu.SemaphoreType.DMA((2,)),
        ],
    )
    return mixed.reshape(patches.shape)


def solution(mesh):
    return jax.shard_map(
        on_device,
        mesh=mesh,
        in_specs=(P("rows", "cols", None), P("rows", "cols")) + (P(),) * 13,
        out_specs=P("rows", "cols", None),
        check_vma=False,
    )
```

```python
import functools

import jax
import jax.numpy as jnp
from jax import lax
from jax.experimental import pallas as pl
from jax.experimental.pallas import tpu as pltpu
from jax.sharding import PartitionSpec as P

bf16, f32 = jnp.bfloat16, jnp.float32
LANES = 128
CAP = 80.0
LOG2E = 1.4426950408889634
FIRST_DOWN = 46
FIRST_BACK = 46


def iota(shape, dim):
    return lax.broadcasted_iota(jnp.int32, shape, dim)


def dot(a, b):
    return jnp.dot(a, b, preferred_element_type=f32)


def dot_t(a, b):
    return lax.dot_general(a, b, (((1,), (1,)), ((), ())), preferred_element_type=f32)


def halves(x):
    high = x.astype(bf16)
    return high, (x - high.astype(f32)).astype(bf16)


def softplus(v):
    return jnp.maximum(v, 0.0) + jnp.log1p(jnp.exp(-jnp.abs(v)))


def dot3(a, b):
    (ah, al), (bh, bl) = halves(a), halves(b)
    return dot(ah, bh) + (dot(al, bh) + dot(ah, bl))


def by_ones(a, ones):
    high, rest = a.astype(bf16), None
    rest = a - high.astype(f32)
    middle = rest.astype(bf16)
    low = (rest - middle.astype(f32)).astype(bf16)
    n = a.shape[0]
    whole = dot(jnp.concatenate([high.astype(f32), middle.astype(f32), low.astype(f32)], axis=0).astype(bf16), ones)
    return whole[:n] + (whole[n : 2 * n] + whole[2 * n :])


def as_column(row):
    n = row.shape[-1]
    square = jnp.broadcast_to(row, (n, n))
    return jnp.sum(jnp.where(iota((n, n), 0) == iota((n, n), 1), square, 0.0), axis=1, keepdims=True)


def head_lanes(head_count, width):
    shape = (head_count, head_count * width)
    return jnp.where(iota(shape, 1) // width == iota(shape, 0), 1.0, 0.0)


def step_terms(proj_rows, bias, rates, group):
    head_count = bias.shape[-1]
    steps = softplus(proj_rows[-head_count:] + as_column(bias))
    falls = -steps * as_column(rates * LOG2E)
    logs = jnp.log(steps) * LOG2E
    blocks = proj_rows.shape[1] // LANES
    stack = lambda x: jnp.concatenate([x[:, k * LANES : (k + 1) * LANES] for k in range(blocks)], axis=0)
    falls, logs = stack(falls), stack(logs)
    source, target = iota((LANES, LANES), 0), iota((LANES, LANES), 1)
    same = source // group == target // group
    running = by_ones(falls, jnp.where(same & (source <= target), 1.0, 0.0).astype(bf16))
    totals = by_ones(falls, jnp.where(same, 1.0, 0.0).astype(bf16))
    return running, running - logs, totals


def products(proj_block, b_block):
    state_count = b_block.shape[0]
    rest = proj_block.shape[1] - 2 * state_count
    padded = jnp.concatenate(
        [jnp.zeros_like(b_block), b_block, jnp.zeros((rest, b_block.shape[1]), f32)], axis=0
    )
    return dot3(proj_block, padded)


def within(proj_block, b_block, group, run_col, less_row, values, block, head_count):
    source, target = iota((LANES, LANES), 1), iota((LANES, LANES), 0)
    keep = (source // group == target // group) & (source <= target)
    inter = jnp.where(keep, products(proj_block, b_block), 0.0)
    low_lanes = iota((LANES, LANES), 1) < LANES // 2
    tiles = []
    for pair in range(head_count // 2):
        weights = []
        for head in (2 * pair, 2 * pair + 1):
            at = block * head_count + head
            spans = run_col[:, at : at + 1] - less_row[at : at + 1, :]
            weights.append((jnp.exp2(jnp.minimum(spans, CAP)) * inter).astype(bf16))
        both = dot(jnp.concatenate(weights, axis=0), values[:, pair * LANES : (pair + 1) * LANES])
        tiles.append(jnp.where(low_lanes, both[:LANES], both[LANES:]))
    return jnp.concatenate(tiles, axis=1)


def pushes(b_block, to_end, group, values, block, head_count):
    state_count = b_block.shape[0]
    groups = LANES // group
    lane = iota((state_count, LANES), 1)
    tiles = [[] for _ in range(groups)]
    for pair in range(head_count // 2):
        rows = []
        for g in range(groups):
            for head in (2 * pair, 2 * pair + 1):
                at = block * head_count + head
                coef = b_block * to_end[at : at + 1, :]
                rows.append(jnp.where(lane // group == g, coef, 0.0).astype(bf16))
        left = dot(jnp.concatenate(rows, axis=0), values[:, pair * LANES : (pair + 1) * LANES])
        for g in range(groups):
            top = left[2 * g * state_count : (2 * g + 1) * state_count]
            bottom = left[(2 * g + 1) * state_count : (2 * g + 2) * state_count]
            tiles[g].append(jnp.where(lane < LANES // 2, top, bottom))
    return [jnp.concatenate(t, axis=1) for t in tiles]


def fetch(sources, targets, sems):
    copies = [
        pltpu.make_async_copy(source, target, sems.at[i])
        for i, (source, target) in enumerate(zip(sources, targets))
    ]
    for copy in copies:
        copy.start()
    return copies


def prepare(*refs):
    patches, tissue, w_value, w_proj, bias, rates = refs[:6]
    masked, values, b_rows, run_row, less_row, payload = refs[6:12]
    patches_in, tissue_in, value_in, proj_in, bias_in, rates_in, sems = refs[12:]
    copies = fetch(
        (tissue, patches, w_proj, bias, rates, w_value),
        (tissue_in, patches_in, proj_in, bias_in, rates_in, value_in),
        sems,
    )
    line_count, width = tissue_in.shape
    head_count = bias_in.shape[-1]
    copies[0].wait()
    flags = jnp.transpose(tissue_in[...].astype(f32))
    copies[1].wait()
    for r in range(line_count):
        keep = jnp.broadcast_to(flags[:, r : r + 1], (width, patches_in.shape[1])).astype(bf16)
        rows = slice(r * width, (r + 1) * width)
        masked[rows, :] = patches_in[rows, :] * keep
    inputs = masked[...]
    for copy in copies[2:5]:
        copy.wait()
    proj_rows = dot_t(proj_in[...], inputs)
    state_count = b_rows.shape[0]
    b_rows[...] = proj_rows[:state_count]
    running, less, totals = step_terms(proj_rows, bias_in[...], rates_in[...], width)
    less_row[...] = less
    run_row[...] = running
    to_end = jnp.exp2(totals - less)
    total_cols = jnp.transpose(totals)
    blocks = inputs.shape[0] // LANES
    groups = LANES // width
    shape = (line_count, blocks * head_count)
    line, column = iota(shape, 0), iota(shape, 1)
    picked = jnp.zeros(shape, f32)
    for g in range(groups):
        here = (line % groups == g) & (column // head_count == line // groups)
        picked = jnp.where(here, total_cols[g * width : g * width + 1, :], picked)
    lanes = jnp.concatenate([head_lanes(head_count, inputs.shape[1] // head_count)] * blocks, axis=0)
    decays = jnp.exp2(by_ones(picked, lanes.astype(bf16)))
    keep_decays(payload, decays)
    copies[5].wait()
    narrow = dot(inputs, value_in[...]).astype(bf16)
    values[...] = narrow
    for k in range(blocks):
        at = slice(k * LANES, (k + 1) * LANES)
        left = pushes(proj_rows[:state_count, at], to_end, width, narrow[at], k, head_count)
        for g in range(groups):
            r = k * groups + g
            payload[r * state_count : (r + 1) * state_count, :] = left[g].astype(bf16)


def keep_decays(payload, decays):
    high, low = halves(decays)
    pair = jnp.concatenate([high.astype(f32), low.astype(f32)], axis=0).astype(bf16)
    payload[payload.shape[0] - pair.shape[0] :, :] = pair


def read_decays(payload, line_count):
    pair = payload[payload.shape[0] - 2 * line_count :, :].astype(f32)
    return pair[:line_count] + pair[line_count:]


def line_rows(r, state_count):
    return slice(r * state_count, (r + 1) * state_count)


def first_step(own, came, state, span, sent):
    line_count = span.shape[0]
    state_count = state.shape[0] // line_count
    later = lax.rem(lax.axis_index("cols"), 2) == 1
    mine, other = read_decays(own, line_count), read_decays(came, line_count)
    span[...] = jnp.where(later, other, 1.0)
    keep_decays(sent, mine * other)
    second = jnp.where(later, mine, other)
    for r in range(line_count):
        at = line_rows(r, state_count)
        here, there = own[at, :].astype(f32), came[at, :].astype(f32)
        state[at, :] = jnp.where(later, there, 0.0)
        head, tail = jnp.where(later, there, here), jnp.where(later, here, there)
        sent[at, :] = (tail + second[r : r + 1] * head).astype(bf16)


def second_step(own, came, state, span, states, spans, sent):
    line_count = span.shape[0]
    state_count = state.shape[0] // line_count
    decays, before = read_decays(own, line_count), read_decays(came, line_count)
    over = span[...]
    spans[...] = over * before
    for r in range(line_count):
        at = line_rows(r, state_count)
        entered = came[at, :].astype(f32)
        states[at, :] = state[at, :] + over[r : r + 1] * entered
        sent[at, :] = (own[at, :].astype(f32) + decays[r : r + 1] * entered).astype(bf16)


def spread(row, lanes):
    return by_ones(jnp.broadcast_to(row, (8, row.shape[-1])), lanes.astype(bf16))[:1]


def make_within(group):
    def body(values, proj, b_rows, run_row, less_row, skips, *refs):
        given, (outputs, reach), passed = refs[:4], refs[4:6], refs[6:]
        run_col = jnp.transpose(run_row[...])
        for source, target in zip(given, passed):
            target[...] = source[...]
        head_count = skips.shape[-1]
        count, width_all = values.shape
        skip = spread(skips[...], head_lanes(head_count, width_all // head_count))
        for k in range(count // LANES):
            at = slice(k * LANES, (k + 1) * LANES)
            block = values[at, :]
            own = within(
                proj[at, :], b_rows[:, at], group, run_col, less_row[...], block, k, head_count
            )
            outputs[at, :] = own + skip * block.astype(f32)
            reach[at, :] = reach_lanes(run_col, k, head_count, width_all)

    return body


def reach_lanes(run_col_block, block, head_count, width_all):
    shape = (run_col_block.shape[1], width_all)
    row, lane = iota(shape, 0), iota(shape, 1)
    here = (row // head_count == block) & (row % head_count == lane // (width_all // head_count))
    lanes = jnp.where(here, 1.0, 0.0).astype(bf16)
    high, low = halves(jnp.exp2(run_col_block))
    return dot(high, lanes) + dot(low, lanes)


def normed(values, gain):
    square = jnp.mean(values * values, axis=-1, keepdims=True)
    return values * lax.rsqrt(square + 1e-05) * gain


def swap_matrix(count, inner, turn=0):
    outer = count // inner
    place, source = iota((count, count), 0), iota((count, count), 1)
    return jnp.where(((place + turn) % outer) * inner + place // outer == source, 1.0, 0.0).astype(bf16)


def finish_rows(outputs, reach, proj, states, spans, came, gain, swap, lines):
    line_count, width_all = spans.shape
    state_count = states.shape[0] // line_count
    count = outputs.shape[0]
    width = count // line_count
    head_count = proj.shape[1] - 2 * state_count
    done = []
    for r in range(line_count):
        at = line_rows(r, state_count)
        state = states[at, :] + spans[r : r + 1, :] * came[at, :].astype(f32)
        padded = jnp.concatenate(
            [
                jnp.zeros((state_count, width_all), f32),
                state,
                jnp.zeros((head_count, width_all), f32),
            ],
            axis=0,
        )
        rows = slice(r * width, (r + 1) * width)
        whole = outputs[rows, :] + dot3(proj[rows, :], padded) * reach[rows, :]
        done.append(normed(whole, gain[...]).astype(bf16))
    lines[...] = dot(swap[...], jnp.concatenate(done, axis=0)).astype(bf16)


def put_turned(ref, start, rows):
    count, here = ref.shape[0], start % ref.shape[0]
    fits = min(count - here, rows.shape[0])
    ref[here : here + fits, :] = rows[:fits]
    if fits < rows.shape[0]:
        ref[: rows.shape[0] - fits, :] = rows[fits:]


def scan_columns(first, last, lines, w_proj, bias, rates, skips, outputs):
    count, width_all = lines.shape
    head_count = bias.shape[-1]
    inputs = lines[...]
    if first:
        inputs = jnp.concatenate([inputs[count - first :], inputs[: count - first]], axis=0)
    proj = dot_t(inputs, w_proj[...])
    proj_rows = dot_t(w_proj[...], inputs)
    state_count = (proj.shape[1] - head_count) // 2
    running, less, totals = step_terms(proj_rows, bias[...], rates[...], LANES)
    run_col = jnp.transpose(running)
    to_end = jnp.exp2(totals - less)
    total_cols = jnp.transpose(totals)
    lanes = head_lanes(head_count, width_all // head_count)
    skip = spread(skips[...], lanes)
    blocks = count // LANES
    shape = (8, blocks * head_count)
    here = iota(shape, 1) // head_count == iota(shape, 0)
    picked = jnp.where(here, jnp.broadcast_to(total_cols[:1], shape), 0.0)
    decays = jnp.exp2(by_ones(picked, jnp.concatenate([lanes] * blocks, axis=0).astype(bf16)))
    state = jnp.zeros((state_count, width_all), f32)
    for k in range(blocks):
        at = slice(k * LANES, (k + 1) * LANES)
        block = inputs[at]
        b_block = proj_rows[:state_count, at]
        own = within(proj[at], b_block, LANES, run_col, less, block, k, head_count)
        own = own + skip * block.astype(f32)
        if k > 0:
            padded = jnp.concatenate(
                [
                    jnp.zeros((state_count, width_all), f32),
                    state,
                    jnp.zeros((head_count, width_all), f32),
                ],
                axis=0,
            )
            own = own + dot3(proj[at], padded) * reach_lanes(
                run_col, k, head_count, width_all
            )
        put_turned(outputs, k * LANES - last, own.astype(bf16))
        if k + 1 < blocks:
            left = pushes(b_block, to_end, LANES, block, k, head_count)[0]
            state = decays[k : k + 1] * state + left


def make_gate(width, turn):
    def gate(masked, w_gate, w_proj, gain, gates, proj, swap, back):
        proj[...] = dot_t(masked[...], w_proj[...])
        value = dot(masked[...], w_gate[...])
        gates[...] = gain[...] * (value / (1.0 + jnp.exp(-value)))
        count = masked.shape[0]
        swap[...] = swap_matrix(count, width)
        back[...] = swap_matrix(count, count // width, turn)

    return gate


def finish(columns, gates, masked, w_out, back, mixed, rows_out, sems):
    act = normed(dot(back[...], columns[...]), gates[...]).astype(bf16)
    copies = []
    part = mixed.shape[1] // sems.shape[0]
    for k in range(sems.shape[0]):
        at = slice(k * part, (k + 1) * part)
        rows_out[:, at] = (masked[:, at].astype(f32) + dot(act, w_out[:, at])).astype(bf16)
        copies.append(pltpu.make_async_copy(rows_out.at[:, at], mixed.at[:, at], sems.at[k]))
        copies[-1].start()
    for copy in copies:
        copy.wait()


def shifted(value, axis, by):
    count = lax.axis_size(axis)
    return lax.ppermute(value, axis, [(i, i + by) for i in range(count - by)])


IN_VMEM = pl.BlockSpec(memory_space=pltpu.VMEM)
IN_PLACE = pl.BlockSpec(memory_space=pltpu.HBM)


def on_core(core, body, skipped=0):
    def guarded(*refs):
        @pl.when(lax.rem(lax.axis_index("cols"), 2) == core)
        def _():
            body(*refs[skipped:])

    return guarded


def call(
    body, out_shape, *args, flops=0, name=None, ins=IN_VMEM, outs=IN_VMEM, scratch=(), aliases={}
):
    single = not isinstance(out_shape, tuple)
    return pl.pallas_call(
        body,
        out_shape=out_shape,
        in_specs=[ins] * len(args),
        out_specs=outs if single else tuple(outs for _ in out_shape),
        scratch_shapes=scratch,
        name=name,
        input_output_aliases=aliases,
        cost_estimate=pl.CostEstimate(flops=flops, bytes_accessed=4 << 20, transcendentals=0),
        compiler_params=pltpu.CompilerParams(vmem_limit_bytes=24 << 20),
    )(*args)


def on_device(
    patches,
    tissue,
    w_value,
    w_across,
    w_down,
    w_gate,
    w_out,
    step_bias_across,
    step_bias_down,
    rates_across,
    rates_down,
    skip_across,
    skip_down,
    gain_across,
    gain_final,
):
    shape = jax.ShapeDtypeStruct
    line_count, width, width_all = patches.shape
    count = line_count * width
    head_count = rates_across.shape[0]
    proj_count = w_across.shape[1]
    state_count = (proj_count - head_count) // 2
    blocks = count // LANES
    row = lambda x: x.reshape(1, -1)
    state_rows = line_count * state_count
    given = (
        patches.reshape(count, width_all),
        tissue,
        w_value,
        w_across.T,
        row(step_bias_across),
        row(rates_across),
    )
    masked, values, b_rows, run_row, less_row, payload = call(
        prepare,
        (
            shape((count, width_all), bf16),
            shape((count, width_all), bf16),
            shape((state_count, count), f32),
            shape((blocks * head_count, LANES), f32),
            shape((blocks * head_count, LANES), f32),
            shape((state_rows + 2 * line_count, width_all), bf16),
        ),
        *(pltpu.with_memory_space_constraint(x, pltpu.HBM) for x in given),
        flops=5 * 10**8,
        name="prepare",
        ins=IN_PLACE,
        scratch=[pltpu.VMEM(x.shape, x.dtype) for x in given]
        + [pltpu.SemaphoreType.DMA((len(given),))],
    )
    count_of = lax.axis_size("cols")
    came = lax.ppermute(payload, "cols", [(i, i ^ 1) for i in range(count_of)])
    state, span, sent = call(
        first_step,
        (
            shape((state_rows, width_all), f32),
            shape((line_count, width_all), f32),
            shape(payload.shape, bf16),
        ),
        payload,
        came,
        flops=10**6,
        name="first_step",
    )
    gate_shapes = (
        shape((count, width_all), f32),
        shape((count, proj_count), f32),
        shape((count, count), bf16),
        shape((count, count), bf16),
    )
    gate = make_gate(width, FIRST_DOWN - FIRST_BACK + width)
    early, _ = lax.optimization_barrier((masked, sent))
    gate_args = (early, w_gate, w_across.T, row(gain_final))
    half_made = call(
        on_core(0, gate), gate_shapes, *gate_args, flops=5 * 10**8, name="gate_first"
    )
    sent, half_made = lax.optimization_barrier((sent, half_made))
    came = shifted(sent, "cols", 2)
    gates, proj, swap, back = call(
        on_core(1, gate, 4),
        gate_shapes,
        *half_made,
        *gate_args,
        flops=5 * 10**8,
        name="gate_second",
        aliases={i: i for i in range(4)},
    )
    came, gates = lax.optimization_barrier((came, gates))
    states, spans, sent = call(
        second_step,
        (
            shape((state_rows, width_all), f32),
            shape((line_count, width_all), f32),
            shape((state_rows, width_all), bf16),
        ),
        sent,
        came,
        state,
        span,
        flops=10**6,
        name="second_step",
    )
    came = shifted(sent, "cols", 4)
    values, _ = lax.optimization_barrier((values, sent))
    passed = tuple(
        row(x) for x in (step_bias_down, rates_down, skip_down, gain_across)
    )
    outputs, reach, bias_down, rate_down, skips_down, gains_across = call(
        make_within(width),
        (shape((count, width_all), f32), shape((count, width_all), f32))
        + tuple(shape(x.shape, x.dtype) for x in passed),
        values,
        proj,
        b_rows,
        run_row,
        less_row,
        row(skip_across),
        *passed,
        flops=10**9,
        name="within_rows",
    )
    lines = call(
        finish_rows,
        shape((count, width_all), bf16),
        outputs,
        reach,
        proj,
        states,
        spans,
        came,
        gains_across,
        swap,
        flops=5 * 10**8,
        name="finish_rows",
    )
    split = (count // line_count, line_count, width_all)
    bands = lax.axis_size("rows")
    order = lambda first: [[(i + first) % bands for i in range(bands)]]
    exchange = lambda x, first: lax.all_to_all(
        x.reshape(split), "rows", 0, 0, axis_index_groups=order(first), tiled=True
    )
    lines = exchange(lines, FIRST_DOWN)
    columns = call(
        functools.partial(scan_columns, FIRST_DOWN * line_count, FIRST_BACK * line_count),
        shape((count, width_all), bf16),
        lines.reshape(count, width_all),
        w_down.T,
        bias_down,
        rate_down,
        skips_down,
        flops=10**9,
        name="scan_columns",
    )
    columns = exchange(columns, FIRST_BACK)
    mixed = call(
        finish,
        shape((count, width_all), bf16),
        columns.reshape(count, width_all),
        gates,
        masked,
        w_out,
        back,
        flops=5 * 10**8,
        name="finish",
        outs=IN_PLACE,
        scratch=[
            pltpu.VMEM((count, width_all), bf16),
            pltpu.SemaphoreType.DMA((2,)),
        ],
    )
    return mixed.reshape(patches.shape)


def solution(mesh):
    return jax.shard_map(
        on_device,
        mesh=mesh,
        in_specs=(P("rows", "cols", None), P("rows", "cols")) + (P(),) * 13,
        out_specs=P("rows", "cols", None),
        check_vma=False,
    )
```

```python
import functools

import jax
import jax.numpy as jnp
from jax import lax
from jax.experimental import pallas as pl
from jax.experimental.pallas import tpu as pltpu
from jax.sharding import PartitionSpec as P

bf16, f32 = jnp.bfloat16, jnp.float32
LANES = 128
CAP = 80.0
FIRST_DOWN = 46
FIRST_BACK = 46


def iota(shape, dim):
    return lax.broadcasted_iota(jnp.int32, shape, dim)


def dot(a, b):
    return jnp.dot(a, b, preferred_element_type=f32)


def dot_t(a, b):
    return lax.dot_general(a, b, (((1,), (1,)), ((), ())), preferred_element_type=f32)


def halves(x):
    high = x.astype(bf16)
    return high, (x - high.astype(f32)).astype(bf16)


def softplus(v):
    return jnp.maximum(v, 0.0) + jnp.log1p(jnp.exp(-jnp.abs(v)))


def dot3(a, b):
    (ah, al), (bh, bl) = halves(a), halves(b)
    return dot(ah, bh) + (dot(al, bh) + dot(ah, bl))


def by_ones(a, ones):
    high, rest = a.astype(bf16), None
    rest = a - high.astype(f32)
    middle = rest.astype(bf16)
    low = (rest - middle.astype(f32)).astype(bf16)
    n = a.shape[0]
    whole = dot(jnp.concatenate([high.astype(f32), middle.astype(f32), low.astype(f32)], axis=0).astype(bf16), ones)
    return whole[:n] + (whole[n : 2 * n] + whole[2 * n :])


def as_column(row):
    n = row.shape[-1]
    square = jnp.broadcast_to(row, (n, n))
    return jnp.sum(jnp.where(iota((n, n), 0) == iota((n, n), 1), square, 0.0), axis=1, keepdims=True)


def head_lanes(head_count, width):
    shape = (head_count, head_count * width)
    return jnp.where(iota(shape, 1) // width == iota(shape, 0), 1.0, 0.0)


def step_terms(proj_rows, bias, rates, group):
    head_count = bias.shape[-1]
    steps = softplus(proj_rows[-head_count:] + as_column(bias))
    falls = -steps * as_column(rates)
    logs = jnp.log(steps)
    blocks = proj_rows.shape[1] // LANES
    stack = lambda x: jnp.concatenate([x[:, k * LANES : (k + 1) * LANES] for k in range(blocks)], axis=0)
    falls, logs = stack(falls), stack(logs)
    source, target = iota((LANES, LANES), 0), iota((LANES, LANES), 1)
    same = source // group == target // group
    running = by_ones(falls, jnp.where(same & (source <= target), 1.0, 0.0).astype(bf16))
    totals = by_ones(falls, jnp.where(same, 1.0, 0.0).astype(bf16))
    return running, running - logs, totals


def products(proj_block, b_block):
    state_count = b_block.shape[0]
    rest = proj_block.shape[1] - 2 * state_count
    padded = jnp.concatenate(
        [jnp.zeros_like(b_block), b_block, jnp.zeros((rest, b_block.shape[1]), f32)], axis=0
    )
    return dot3(proj_block, padded)


def within(proj_block, b_block, group, run_col, less_row, values, block, head_count):
    source, target = iota((LANES, LANES), 1), iota((LANES, LANES), 0)
    keep = (source // group == target // group) & (source <= target)
    inter = jnp.where(keep, products(proj_block, b_block), 0.0)
    low_lanes = iota((LANES, LANES), 1) < LANES // 2
    tiles = []
    for pair in range(head_count // 2):
        weights = []
        for head in (2 * pair, 2 * pair + 1):
            at = block * head_count + head
            spans = run_col[:, at : at + 1] - less_row[at : at + 1, :]
            weights.append((jnp.exp(jnp.minimum(spans, CAP)) * inter).astype(bf16))
        both = dot(jnp.concatenate(weights, axis=0), values[:, pair * LANES : (pair + 1) * LANES])
        tiles.append(jnp.where(low_lanes, both[:LANES], both[LANES:]))
    return jnp.concatenate(tiles, axis=1)


def pushes(b_block, to_end, group, values, block, head_count):
    state_count = b_block.shape[0]
    groups = LANES // group
    lane = iota((state_count, LANES), 1)
    tiles = [[] for _ in range(groups)]
    for pair in range(head_count // 2):
        rows = []
        for g in range(groups):
            for head in (2 * pair, 2 * pair + 1):
                at = block * head_count + head
                coef = b_block * to_end[at : at + 1, :]
                rows.append(jnp.where(lane // group == g, coef, 0.0).astype(bf16))
        left = dot(jnp.concatenate(rows, axis=0), values[:, pair * LANES : (pair + 1) * LANES])
        for g in range(groups):
            top = left[2 * g * state_count : (2 * g + 1) * state_count]
            bottom = left[(2 * g + 1) * state_count : (2 * g + 2) * state_count]
            tiles[g].append(jnp.where(lane < LANES // 2, top, bottom))
    return [jnp.concatenate(t, axis=1) for t in tiles]


def fetch(sources, targets, sems):
    copies = [
        pltpu.make_async_copy(source, target, sems.at[i])
        for i, (source, target) in enumerate(zip(sources, targets))
    ]
    for copy in copies:
        copy.start()
    return copies


def prepare(*refs):
    patches, tissue, w_value, w_proj, bias, rates = refs[:6]
    masked, values, b_rows, run_row, less_row, payload = refs[6:12]
    patches_in, tissue_in, value_in, proj_in, bias_in, rates_in, sems = refs[12:]
    copies = fetch(
        (tissue, patches, w_proj, bias, rates, w_value),
        (tissue_in, patches_in, proj_in, bias_in, rates_in, value_in),
        sems,
    )
    line_count, width = tissue_in.shape
    head_count = bias_in.shape[-1]
    copies[0].wait()
    flags = jnp.transpose(tissue_in[...].astype(f32))
    copies[1].wait()
    for r in range(line_count):
        keep = jnp.broadcast_to(flags[:, r : r + 1], (width, patches_in.shape[1])).astype(bf16)
        rows = slice(r * width, (r + 1) * width)
        masked[rows, :] = patches_in[rows, :] * keep
    inputs = masked[...]
    for copy in copies[2:5]:
        copy.wait()
    proj_rows = dot_t(proj_in[...], inputs)
    state_count = b_rows.shape[0]
    b_rows[...] = proj_rows[:state_count]
    running, less, totals = step_terms(proj_rows, bias_in[...], rates_in[...], width)
    less_row[...] = less
    run_row[...] = running
    to_end = jnp.exp(totals - less)
    total_cols = jnp.transpose(totals)
    blocks = inputs.shape[0] // LANES
    groups = LANES // width
    shape = (line_count, blocks * head_count)
    line, column = iota(shape, 0), iota(shape, 1)
    picked = jnp.zeros(shape, f32)
    for g in range(groups):
        here = (line % groups == g) & (column // head_count == line // groups)
        picked = jnp.where(here, total_cols[g * width : g * width + 1, :], picked)
    lanes = jnp.concatenate([head_lanes(head_count, inputs.shape[1] // head_count)] * blocks, axis=0)
    decays = jnp.exp(by_ones(picked, lanes.astype(bf16)))
    keep_decays(payload, decays)
    copies[5].wait()
    narrow = dot(inputs, value_in[...]).astype(bf16)
    values[...] = narrow
    for k in range(blocks):
        at = slice(k * LANES, (k + 1) * LANES)
        left = pushes(proj_rows[:state_count, at], to_end, width, narrow[at], k, head_count)
        for g in range(groups):
            r = k * groups + g
            payload[r * state_count : (r + 1) * state_count, :] = left[g].astype(bf16)


def keep_decays(payload, decays):
    high, low = halves(decays)
    pair = jnp.concatenate([high.astype(f32), low.astype(f32)], axis=0).astype(bf16)
    payload[payload.shape[0] - pair.shape[0] :, :] = pair


def read_decays(payload, line_count):
    pair = payload[payload.shape[0] - 2 * line_count :, :].astype(f32)
    return pair[:line_count] + pair[line_count:]


def line_rows(r, state_count):
    return slice(r * state_count, (r + 1) * state_count)


def first_step(own, came, state, span, sent):
    line_count = span.shape[0]
    state_count = state.shape[0] // line_count
    later = lax.rem(lax.axis_index("cols"), 2) == 1
    mine, other = read_decays(own, line_count), read_decays(came, line_count)
    span[...] = jnp.where(later, other, 1.0)
    keep_decays(sent, mine * other)
    second = jnp.where(later, mine, other)
    for r in range(line_count):
        at = line_rows(r, state_count)
        here, there = own[at, :].astype(f32), came[at, :].astype(f32)
        state[at, :] = jnp.where(later, there, 0.0)
        head, tail = jnp.where(later, there, here), jnp.where(later, here, there)
        sent[at, :] = (tail + second[r : r + 1] * head).astype(bf16)


def second_step(own, came, state, span, states, spans, sent):
    line_count = span.shape[0]
    state_count = state.shape[0] // line_count
    decays, before = read_decays(own, line_count), read_decays(came, line_count)
    over = span[...]
    spans[...] = over * before
    for r in range(line_count):
        at = line_rows(r, state_count)
        entered = came[at, :].astype(f32)
        states[at, :] = state[at, :] + over[r : r + 1] * entered
        sent[at, :] = (own[at, :].astype(f32) + decays[r : r + 1] * entered).astype(bf16)


def spread(row, lanes):
    return by_ones(jnp.broadcast_to(row, (8, row.shape[-1])), lanes.astype(bf16))[:1]


def make_within(group):
    def body(values, proj, b_rows, run_row, less_row, skips, *refs):
        given, (outputs, reach), passed = refs[:4], refs[4:6], refs[6:]
        run_col = jnp.transpose(run_row[...])
        for source, target in zip(given, passed):
            target[...] = source[...]
        head_count = skips.shape[-1]
        count, width_all = values.shape
        skip = spread(skips[...], head_lanes(head_count, width_all // head_count))
        for k in range(count // LANES):
            at = slice(k * LANES, (k + 1) * LANES)
            block = values[at, :]
            own = within(
                proj[at, :], b_rows[:, at], group, run_col, less_row[...], block, k, head_count
            )
            outputs[at, :] = own + skip * block.astype(f32)
            reach[at, :] = reach_lanes(run_col, k, head_count, width_all)

    return body


def reach_lanes(run_col_block, block, head_count, width_all):
    shape = (run_col_block.shape[1], width_all)
    row, lane = iota(shape, 0), iota(shape, 1)
    here = (row // head_count == block) & (row % head_count == lane // (width_all // head_count))
    lanes = jnp.where(here, 1.0, 0.0).astype(bf16)
    high, low = halves(jnp.exp(run_col_block))
    return dot(high, lanes) + dot(low, lanes)


def normed(values, gain):
    square = jnp.mean(values * values, axis=-1, keepdims=True)
    return values * lax.rsqrt(square + 1e-05) * gain


def swap_matrix(count, inner, turn=0):
    outer = count // inner
    place, source = iota((count, count), 0), iota((count, count), 1)
    return jnp.where(((place + turn) % outer) * inner + place // outer == source, 1.0, 0.0).astype(bf16)


def finish_rows(outputs, reach, proj, states, spans, came, gain, swap, lines):
    line_count, width_all = spans.shape
    state_count = states.shape[0] // line_count
    count = outputs.shape[0]
    width = count // line_count
    head_count = proj.shape[1] - 2 * state_count
    done = []
    for r in range(line_count):
        at = line_rows(r, state_count)
        state = states[at, :] + spans[r : r + 1, :] * came[at, :].astype(f32)
        padded = jnp.concatenate(
            [
                jnp.zeros((state_count, width_all), f32),
                state,
                jnp.zeros((head_count, width_all), f32),
            ],
            axis=0,
        )
        rows = slice(r * width, (r + 1) * width)
        whole = outputs[rows, :] + dot3(proj[rows, :], padded) * reach[rows, :]
        done.append(normed(whole, gain[...]).astype(bf16))
    lines[...] = dot(swap[...], jnp.concatenate(done, axis=0)).astype(bf16)


def put_turned(ref, start, rows):
    count, here = ref.shape[0], start % ref.shape[0]
    fits = min(count - here, rows.shape[0])
    ref[here : here + fits, :] = rows[:fits]
    if fits < rows.shape[0]:
        ref[: rows.shape[0] - fits, :] = rows[fits:]


def scan_columns(first, last, lines, w_proj, bias, rates, skips, outputs):
    count, width_all = lines.shape
    head_count = bias.shape[-1]
    inputs = lines[...]
    if first:
        inputs = jnp.concatenate([inputs[count - first :], inputs[: count - first]], axis=0)
    proj = dot_t(inputs, w_proj[...])
    proj_rows = dot_t(w_proj[...], inputs)
    state_count = (proj.shape[1] - head_count) // 2
    running, less, totals = step_terms(proj_rows, bias[...], rates[...], LANES)
    run_col = jnp.transpose(running)
    to_end = jnp.exp(totals - less)
    total_cols = jnp.transpose(totals)
    lanes = head_lanes(head_count, width_all // head_count)
    skip = spread(skips[...], lanes)
    blocks = count // LANES
    shape = (8, blocks * head_count)
    here = iota(shape, 1) // head_count == iota(shape, 0)
    picked = jnp.where(here, jnp.broadcast_to(total_cols[:1], shape), 0.0)
    decays = jnp.exp(by_ones(picked, jnp.concatenate([lanes] * blocks, axis=0).astype(bf16)))
    state = jnp.zeros((state_count, width_all), f32)
    for k in range(blocks):
        at = slice(k * LANES, (k + 1) * LANES)
        block = inputs[at]
        b_block = proj_rows[:state_count, at]
        own = within(proj[at], b_block, LANES, run_col, less, block, k, head_count)
        own = own + skip * block.astype(f32)
        if k > 0:
            padded = jnp.concatenate(
                [
                    jnp.zeros((state_count, width_all), f32),
                    state,
                    jnp.zeros((head_count, width_all), f32),
                ],
                axis=0,
            )
            own = own + dot3(proj[at], padded) * reach_lanes(
                run_col, k, head_count, width_all
            )
        put_turned(outputs, k * LANES - last, own.astype(bf16))
        if k + 1 < blocks:
            left = pushes(b_block, to_end, LANES, block, k, head_count)[0]
            state = decays[k : k + 1] * state + left


def make_gate(width, turn):
    def gate(masked, w_gate, w_proj, gain, gates, proj, swap, back):
        proj[...] = dot_t(masked[...], w_proj[...])
        value = dot(masked[...], w_gate[...])
        gates[...] = gain[...] * (value / (1.0 + jnp.exp(-value)))
        count = masked.shape[0]
        swap[...] = swap_matrix(count, width)
        back[...] = swap_matrix(count, count // width, turn)

    return gate


def finish(columns, gates, masked, w_out, back, mixed, rows_out, sems):
    act = normed(dot(back[...], columns[...]), gates[...]).astype(bf16)
    copies = []
    part = mixed.shape[1] // sems.shape[0]
    for k in range(sems.shape[0]):
        at = slice(k * part, (k + 1) * part)
        rows_out[:, at] = (masked[:, at].astype(f32) + dot(act, w_out[:, at])).astype(bf16)
        copies.append(pltpu.make_async_copy(rows_out.at[:, at], mixed.at[:, at], sems.at[k]))
        copies[-1].start()
    for copy in copies:
        copy.wait()


def shifted(value, axis, by):
    count = lax.axis_size(axis)
    return lax.ppermute(value, axis, [(i, i + by) for i in range(count - by)])


IN_VMEM = pl.BlockSpec(memory_space=pltpu.VMEM)
IN_PLACE = pl.BlockSpec(memory_space=pltpu.HBM)


def on_core(core, body, skipped=0):
    def guarded(*refs):
        @pl.when(lax.rem(lax.axis_index("cols"), 2) == core)
        def _():
            body(*refs[skipped:])

    return guarded


def call(
    body, out_shape, *args, flops=0, name=None, ins=IN_VMEM, outs=IN_VMEM, scratch=(), aliases={}
):
    single = not isinstance(out_shape, tuple)
    return pl.pallas_call(
        body,
        out_shape=out_shape,
        in_specs=[ins] * len(args),
        out_specs=outs if single else tuple(outs for _ in out_shape),
        scratch_shapes=scratch,
        name=name,
        input_output_aliases=aliases,
        cost_estimate=pl.CostEstimate(flops=flops, bytes_accessed=4 << 20, transcendentals=0),
        compiler_params=pltpu.CompilerParams(vmem_limit_bytes=24 << 20),
    )(*args)


def on_device(
    patches,
    tissue,
    w_value,
    w_across,
    w_down,
    w_gate,
    w_out,
    step_bias_across,
    step_bias_down,
    rates_across,
    rates_down,
    skip_across,
    skip_down,
    gain_across,
    gain_final,
):
    shape = jax.ShapeDtypeStruct
    line_count, width, width_all = patches.shape
    count = line_count * width
    head_count = rates_across.shape[0]
    proj_count = w_across.shape[1]
    state_count = (proj_count - head_count) // 2
    blocks = count // LANES
    row = lambda x: x.reshape(1, -1)
    state_rows = line_count * state_count
    given = (
        patches.reshape(count, width_all),
        tissue,
        w_value,
        w_across.T,
        row(step_bias_across),
        row(rates_across),
    )
    masked, values, b_rows, run_row, less_row, payload = call(
        prepare,
        (
            shape((count, width_all), bf16),
            shape((count, width_all), bf16),
            shape((state_count, count), f32),
            shape((blocks * head_count, LANES), f32),
            shape((blocks * head_count, LANES), f32),
            shape((state_rows + 2 * line_count, width_all), bf16),
        ),
        *(pltpu.with_memory_space_constraint(x, pltpu.HBM) for x in given),
        flops=5 * 10**8,
        name="prepare",
        ins=IN_PLACE,
        scratch=[pltpu.VMEM(x.shape, x.dtype) for x in given]
        + [pltpu.SemaphoreType.DMA((len(given),))],
    )
    count_of = lax.axis_size("cols")
    came = lax.ppermute(payload, "cols", [(i, i ^ 1) for i in range(count_of)])
    state, span, sent = call(
        first_step,
        (
            shape((state_rows, width_all), f32),
            shape((line_count, width_all), f32),
            shape(payload.shape, bf16),
        ),
        payload,
        came,
        flops=10**6,
        name="first_step",
    )
    gate_shapes = (
        shape((count, width_all), f32),
        shape((count, proj_count), f32),
        shape((count, count), bf16),
        shape((count, count), bf16),
    )
    gate = make_gate(width, FIRST_DOWN - FIRST_BACK + width)
    early, _ = lax.optimization_barrier((masked, sent))
    gate_args = (early, w_gate, w_across.T, row(gain_final))
    half_made = call(
        on_core(0, gate), gate_shapes, *gate_args, flops=5 * 10**8, name="gate_first"
    )
    sent, half_made = lax.optimization_barrier((sent, half_made))
    came = shifted(sent, "cols", 2)
    gates, proj, swap, back = call(
        on_core(1, gate, 4),
        gate_shapes,
        *half_made,
        *gate_args,
        flops=5 * 10**8,
        name="gate_second",
        aliases={i: i for i in range(4)},
    )
    came, gates = lax.optimization_barrier((came, gates))
    states, spans, sent = call(
        second_step,
        (
            shape((state_rows, width_all), f32),
            shape((line_count, width_all), f32),
            shape((state_rows, width_all), bf16),
        ),
        sent,
        came,
        state,
        span,
        flops=10**6,
        name="second_step",
    )
    came = shifted(sent, "cols", 4)
    values, _ = lax.optimization_barrier((values, sent))
    passed = tuple(
        row(x) for x in (step_bias_down, rates_down, skip_down, gain_across)
    )
    outputs, reach, bias_down, rate_down, skips_down, gains_across = call(
        make_within(width),
        (shape((count, width_all), f32), shape((count, width_all), f32))
        + tuple(shape(x.shape, x.dtype) for x in passed),
        values,
        proj,
        b_rows,
        run_row,
        less_row,
        row(skip_across),
        *passed,
        flops=10**9,
        name="within_rows",
    )
    lines = call(
        finish_rows,
        shape((count, width_all), bf16),
        outputs,
        reach,
        proj,
        states,
        spans,
        came,
        gains_across,
        swap,
        flops=5 * 10**8,
        name="finish_rows",
    )
    split = (count // line_count, line_count, width_all)
    bands = lax.axis_size("rows")
    order = lambda first: [[(i + first) % bands for i in range(bands)]]
    exchange = lambda x, first: lax.all_to_all(
        x.reshape(split), "rows", 0, 0, axis_index_groups=order(first), tiled=True
    )
    lines = exchange(lines, FIRST_DOWN)
    columns = call(
        functools.partial(scan_columns, FIRST_DOWN * line_count, FIRST_BACK * line_count),
        shape((count, width_all), bf16),
        lines.reshape(count, width_all),
        w_down.T,
        bias_down,
        rate_down,
        skips_down,
        flops=10**9,
        name="scan_columns",
    )
    columns = exchange(columns, FIRST_BACK)
    mixed = call(
        finish,
        shape((count, width_all), bf16),
        columns.reshape(count, width_all),
        gates,
        masked,
        w_out,
        back,
        flops=5 * 10**8,
        name="finish",
        outs=IN_PLACE,
        scratch=[
            pltpu.VMEM((count, width_all), bf16),
            pltpu.SemaphoreType.DMA((4,)),
        ],
    )
    return mixed.reshape(patches.shape)


def solution(mesh):
    return jax.shard_map(
        on_device,
        mesh=mesh,
        in_specs=(P("rows", "cols", None), P("rows", "cols")) + (P(),) * 13,
        out_specs=P("rows", "cols", None),
        check_vma=False,
    )
```
